256 devices in a mesh: dp: 8 (over y, core), expert: 32 (over x, z).
Axes of the slice: x: 4, y: 4, z: 8, core: 2. Of those that a mesh axis runs over, the one named last changes fastest.
Arguments:
- tokens: bfloat16 [8192, 3584], P('expert', 'dp'), may hold values from -6 to 6
- cotangent: bfloat16 [8192, 3584], P('expert', 'dp'), may hold values from -6 to 6
- slot_tokens: int32 [32, 32, 32], P('expert'), may hold values from 0 to 255
- slot_counts: int32 [32, 32], P('expert'), may hold values from 0 to 32, as said below
- slot_gates: float32 [32, 32, 32], P('expert'), may hold values from 0.1 to 1
- swap_pairs: int32 [16], replicated, may hold values from 0 to 1, as said below
- gate_weight: bfloat16 [32, 3584, 1024], P('expert', 'dp'), may hold values from -0.09375 to 0.09375
- up_weight: bfloat16 [32, 3584, 1024], P('expert', 'dp'), may hold values from -0.09375 to 0.09375
- down_weight: bfloat16 [32, 1024, 3584], P('expert', None, 'dp'), may hold values from -0.1875 to 0.1875
- first_moment: float32 [32, 1024, 3584], P('expert', None, 'dp'), may hold values from -6 to 6
- second_moment: float32 [32, 1024, 3584], P('expert', None, 'dp'), may hold values from 0.5 to 4
Outputs:
- mixed: bfloat16 [8192, 3584], P('expert', 'dp')
- token_grad: bfloat16 [8192, 3584], P('expert', 'dp')
- new_first_moment: float32 [32, 1024, 3584], P('expert', None, 'dp')
- new_second_moment: float32 [32, 1024, 3584], P('expert', None, 'dp')
- adam_step: bfloat16 [32, 1024, 3584], P('expert', None, 'dp')
The draws below stay inside these ranges and needn't reach their ends.
Inputs may be any that keep to these rules, and one draw needn't show every extreme that they name: `slot_tokens`: slots at or past slot_counts hold arbitrary token numbers and carry nothing. `slot_counts`: every source fills all 32 slots of some expert, and one expert receives 32 live slots from every source. `swap_pairs`: at least one pair trades and at least one pair does not.
All inputs are finite; a program needn't handle non-finite values.
Results may differ from the reference program's by a relative error of at most 0.022.
Values may be sent and summed in bfloat16 or wider, within the bound.
No kernel may reach another device: no remote copies, remote signals or barrier semaphores. Data moves between devices by JAX's collectives and lax.ppermute only.
A program may use at most 128 MiB of HBM per device.

```python
import math
import jax
import jax.numpy as jnp
from jax import lax

D = 3584
FFW = 1024
CAP = 32
TOK = 256
EXPERTS = 32
N_DP = 8
N_EXPERT = 32


def draw_slot_counts(key, part):
    key_heat, key_fill, key_full, key_pick = jax.random.split(jax.random.fold_in(key, 11), 4)
    heat = jax.random.randint(key_heat, (EXPERTS,), 1, 4)
    ceiling = heat * CAP // 3
    counts = jax.random.randint(key_fill, (EXPERTS, EXPERTS), 0, CAP + 1)
    counts = counts * ceiling[None, :] // CAP
    columns = jnp.arange(EXPERTS)
    full_expert = jax.random.randint(key_full, (), 0, EXPERTS)
    counts = jnp.where(columns[None, :] == full_expert, CAP, counts)
    picked = jax.random.randint(key_pick, (EXPERTS,), 0, EXPERTS)
    counts = jnp.where(columns[None, :] == picked[:, None], CAP, counts)
    return counts.astype(jnp.int32)


def draw_swap_pairs(key, part):
    key_flags, key_force, key_keep = jax.random.split(jax.random.fold_in(key, 23), 3)
    half_count = EXPERTS // 2
    flags = jax.random.randint(key_flags, (half_count,), 0, 2)
    forced = jax.random.randint(key_force, (), 0, half_count)
    offset = jax.random.randint(key_keep, (), 1, half_count)
    kept = (forced + offset) % half_count
    places = jnp.arange(half_count)
    flags = jnp.where(places == forced, 1, flags)
    flags = jnp.where(places == kept, 0, flags)
    return flags.astype(jnp.int32)


def set_ends(entries, own_key, smallest, largest):
    extent = entries.shape
    index_at = [jax.random.randint(jax.random.fold_in(own_key, axis), (), 0, extent[axis]) for axis in range(len(extent))]
    entries = entries.at[tuple(index_at)].set(smallest)
    longest = extent.index(max(extent))
    index_at[longest] = (index_at[longest] + 1) % extent[longest]
    return entries.at[tuple(index_at)].set(largest)


def steps_of(rng, shape, cuts, low, top_value):
    factor_of = 1.0
    for position, shards_of in cuts:
        draws = jax.random.uniform(jax.random.fold_in(jax.random.fold_in(rng, 6), position), (shards_of,), jnp.float32, low / len(cuts), top_value / len(cuts))
        factor_of = factor_of * jnp.repeat(jnp.exp(draws), shape[position] // shards_of).reshape((-1,) + (1,) * (len(shape) - 1 - position))
    return factor_of


def gaussian(rng, shape, deviation, bound, pieces=(), held_as=jnp.bfloat16):
    entries = jax.random.normal(rng, shape, jnp.float32) * deviation
    if len(pieces) > 0:
        entries = steps_of(rng, shape, pieces, -0.22, 0.18) * entries
    return jnp.clip(entries, min=-bound, max=bound).astype(held_as)


def setup_inputs(seed: int = 0) -> dict:
    streams_of = jax.random.split(jax.random.key(seed), 12)
    tokens = gaussian(streams_of[0], (N_EXPERT * TOK, D), 1.0, 6.0, ((0, 32), (1, 8)))
    cotangent = gaussian(streams_of[1], (N_EXPERT * TOK, D), 1.0, 6.0, ((0, 32), (1, 8)))
    slot_tokens = set_ends(jax.random.randint(streams_of[2], (N_EXPERT, EXPERTS, CAP), 0, TOK), jax.random.fold_in(streams_of[2], 1), 0, TOK - 1).astype(jnp.int32)
    slot_counts = draw_slot_counts(jax.random.fold_in(streams_of[11], 71), 0)
    slot_gates = jnp.clip(0.1 + 0.9 * jax.random.uniform(streams_of[4], (N_EXPERT, EXPERTS, CAP), jnp.float32) ** steps_of(streams_of[4], (N_EXPERT, EXPERTS, CAP), ((0, 32),), -0.2, 0.2), 0.1, 1.0)
    swap_pairs = draw_swap_pairs(jax.random.fold_in(streams_of[11], 71), 0)
    gate_weight = gaussian(streams_of[6], (EXPERTS, D, FFW), D ** -0.5, 0.09375, ((0, 32), (1, 8)))
    up_weight = gaussian(streams_of[7], (EXPERTS, D, FFW), D ** -0.5, 0.09375, ((0, 32), (1, 8)))
    down_weight = gaussian(streams_of[8], (EXPERTS, FFW, D), FFW ** -0.5, 0.1875, ((0, 32), (2, 8)))
    first_moment = gaussian(streams_of[9], (EXPERTS, FFW, D), 1.0, 6.0, ((0, 32), (2, 8)), jnp.float32)
    second_moment = jnp.clip(jnp.exp(math.log(4.0) - 2.0794415 * jax.random.uniform(streams_of[10], (EXPERTS, FFW, D), jnp.float32) ** steps_of(streams_of[10], (EXPERTS, FFW, D), ((0, 32), (2, 8)), -0.2, 0.2)), 0.5, 4.0)
    return dict(tokens=tokens, cotangent=cotangent, slot_tokens=slot_tokens, slot_counts=slot_counts, slot_gates=slot_gates, swap_pairs=swap_pairs, gate_weight=gate_weight, up_weight=up_weight, down_weight=down_weight, first_moment=first_moment, second_moment=second_moment)


def held_order(values, pair_flags):
    half_count = pair_flags.shape[0]
    blocks = values.reshape((2, half_count) + values.shape[1:])
    chosen = pair_flags.reshape((1, half_count) + (1,) * (values.ndim - 1)) > 0
    return jnp.where(chosen, blocks[::-1], blocks).reshape(values.shape)

def pick_rows(anchor, positions):
    return anchor[positions]

def reference(tokens, cotangent, slot_tokens, slot_counts, slot_gates, swap_pairs, gate_weight, up_weight, down_weight, first_moment, second_moment):
    block_cols = D // N_DP
    row_count = N_EXPERT * CAP
    live_slots = (jnp.arange(CAP)[None, None, :] < slot_counts[:, :, None]).astype(jnp.float32)
    weighted = live_slots * slot_gates
    token_blocks = tokens.reshape(N_EXPERT, TOK, D)
    grad_blocks = cotangent.reshape(N_EXPERT, TOK, D)
    picked = jax.vmap(pick_rows)(token_blocks, slot_tokens)
    picked = jnp.where(live_slots[..., None] > 0, picked, jnp.zeros_like(picked))
    picked_grad = (jax.vmap(pick_rows)(grad_blocks, slot_tokens).astype(jnp.float32) * weighted[..., None]).astype(jnp.bfloat16)
    by_expert = jnp.swapaxes(picked, 0, 1)
    grad_by_expert = jnp.swapaxes(picked_grad, 0, 1)

    def expert_pass(operands):
        rows_in, grads_in, gate_w, up_w, down_w, moment_one, moment_two = operands
        flat_rows = rows_in.reshape(row_count, D)
        gate_up = jnp.concatenate([gate_w, up_w], axis=1)
        partial_pre = jnp.einsum('rkd,kdf->krf', flat_rows.reshape(row_count, N_DP, block_cols).astype(jnp.float32), gate_up.reshape(N_DP, block_cols, 2 * FFW).astype(jnp.float32))
        preact = lax.optimization_barrier(jnp.sum(lax.optimization_barrier(partial_pre.astype(jnp.bfloat16)).astype(jnp.float32), axis=0))
        gate_pre = preact[:, :FFW]
        up_pre = preact[:, FFW:]
        hidden = (jax.nn.silu(gate_pre) * up_pre).astype(jnp.bfloat16)
        outputs = jnp.dot(hidden, down_w, preferred_element_type=jnp.float32).astype(jnp.bfloat16)
        flat_grad = grads_in.reshape(row_count, D)
        weight_grad = jnp.dot(hidden.T, flat_grad, preferred_element_type=jnp.float32)
        partial_hidden = jnp.einsum('rkd,fkd->krf', flat_grad.reshape(row_count, N_DP, block_cols).astype(jnp.float32), down_w.reshape(FFW, N_DP, block_cols).astype(jnp.float32))
        hidden_grad = lax.optimization_barrier(jnp.sum(lax.optimization_barrier(partial_hidden.astype(jnp.bfloat16)).astype(jnp.float32), axis=0))
        sigmoid_gate = jax.nn.sigmoid(gate_pre)
        preact_grad = jnp.concatenate([hidden_grad * up_pre * sigmoid_gate * (1.0 + gate_pre * (1.0 - sigmoid_gate)), hidden_grad * gate_pre * sigmoid_gate], axis=1).astype(jnp.bfloat16)
        input_grad = jnp.dot(preact_grad, gate_up.T, preferred_element_type=jnp.float32).astype(jnp.bfloat16)
        new_one = 0.9 * moment_one + 0.1 * weight_grad
        new_two = 0.999 * moment_two + 0.001 * weight_grad * weight_grad
        step_dir = (new_one / (jnp.sqrt(new_two) + 1e-08)).astype(jnp.bfloat16)
        return (outputs.reshape(N_EXPERT, CAP, D), input_grad.reshape(N_EXPERT, CAP, D), new_one, new_two, step_dir)
    outputs, input_grads, new_one, new_two, step_dir = lax.map(expert_pass, (by_expert, grad_by_expert, gate_weight, up_weight, down_weight, first_moment, second_moment))

    def combine(slot_values, positions, coef):
        return jnp.zeros((TOK, D), jnp.float32).at[positions.reshape(-1)].add(slot_values.reshape(-1, D).astype(jnp.float32) * coef.reshape(-1, 1))
    mixed = jax.vmap(combine)(jnp.swapaxes(outputs, 0, 1), slot_tokens, weighted).reshape(N_EXPERT * TOK, D).astype(jnp.bfloat16)
    token_grad = jax.vmap(combine)(jnp.swapaxes(input_grads, 0, 1), slot_tokens, live_slots).reshape(N_EXPERT * TOK, D).astype(jnp.bfloat16)
    return (mixed, token_grad, held_order(new_one, swap_pairs), held_order(new_two, swap_pairs), held_order(step_dir, swap_pairs))
```

```python
import jax
import jax.numpy as jnp
from jax import lax
from jax.sharding import PartitionSpec as P


beta_first = 0.9
beta_second = 0.999
adam_eps = 1e-08
BF = jnp.bfloat16
F32 = jnp.float32


def dot(a, b, ca=1, cb=0):
    return lax.dot_general(a, b, (((ca,), (cb,)), ((), ())), preferred_element_type=F32)


def core_swap(block):
    return lax.ppermute(block, "dp", [(i, i ^ 1) for i in range(lax.axis_size("dp"))])


def chip_shift(block, step):
    count = lax.axis_size("dp")
    return lax.ppermute(block, "dp", [(i, (i + 2 * step) % count) for i in range(count)])


def expert_swap(block):
    count = lax.axis_size("expert")
    return lax.ppermute(block, "expert", [(i, i ^ (count // 2)) for i in range(count)])


def rows_at(block, index, rows):
    return lax.dynamic_slice_in_dim(block, index * rows, rows, 0)


def tie(value, *others):
    return lax.optimization_barrier((value,) + others)[0]


def pieces_of(keep, other, y_pos, chips):
    rows = keep.shape[0] // chips
    found = []
    for step in range(chips):
        at = (y_pos + step) % chips
        found.append(rows_at(keep, at, rows).astype(F32) + rows_at(other, at, rows).astype(F32))
    return found


def scatter_sum(pieces):
    total = pieces[0]
    for step in range(1, len(pieces)):
        came = chip_shift(pieces[step].astype(BF), step)
        total = total + came.astype(F32)
    return total


def gather_rows(shard, y_pos, core, chips):
    rows = shard.shape[0]
    half = jnp.zeros((chips * rows,) + shard.shape[1:], shard.dtype)
    half = lax.dynamic_update_slice_in_dim(half, shard, y_pos * rows, 0)
    for step in range(1, chips):
        piece = chip_shift(shard, step)
        half = lax.dynamic_update_slice_in_dim(half, piece, ((y_pos - step) % chips) * rows, 0)
    far = core_swap(half)
    full = jnp.where(core == 0, jnp.concatenate([half, far]), jnp.concatenate([far, half]))
    return half, full


def shards(
    tokens,
    cotangent,
    slot_tokens,
    slot_counts,
    slot_gates,
    swap_pairs,
    gate_weight,
    up_weight,
    down_weight,
    first_moment,
    second_moment,
):
    tok_count, model_cols = tokens.shape
    experts = slot_counts.shape[1]
    capacity = slot_tokens.shape[2]
    rows = experts * capacity
    half_rows = rows // 2
    chips = lax.axis_size("dp") // 2
    dp_pos = lax.axis_index("dp")
    core, y_pos = dp_pos % 2, dp_pos // 2
    position = lax.axis_index("expert")
    half_count = swap_pairs.shape[0]
    own_swap = (
        jnp.sum(jnp.where(jnp.arange(half_count) == position % half_count, swap_pairs, 0)) > 0
    )
    down_w = down_weight[0]
    live = (jnp.arange(capacity)[None, :] < slot_counts[0][:, None]).reshape(-1)
    route = slot_tokens[0].reshape(-1)
    weighted = jnp.where(live, slot_gates[0].reshape(-1), 0.0)
    masked_route = jnp.where(live, route, -1)
    token_ids = jnp.arange(tok_count)

    def exchange(block):
        return lax.all_to_all(
            block.reshape(experts, capacity, model_cols), "expert", 0, 0, tiled=True
        ).reshape(rows, model_cols)

    pick = (masked_route[:, None] == token_ids[None, :]).astype(BF)
    arrived = exchange(dot(pick, tokens).astype(BF))
    grad_rows = (dot(pick, cotangent) * weighted[:, None]).astype(BF)
    arrived_grad = exchange(grad_rows)
    far_one = expert_swap(first_moment[0].astype(BF))
    far_two = expert_swap(second_moment[0].astype(BF))
    gate_up = lax.optimization_barrier(jnp.concatenate([gate_weight[0], up_weight[0]], axis=1))

    pre_far = core_swap(dot(rows_at(arrived, 1 - core, half_rows), gate_up).astype(BF))
    pre_own = dot(rows_at(arrived, core, half_rows), gate_up).astype(BF)
    preact = scatter_sum(pieces_of(pre_own, pre_far, y_pos, chips))
    hidden_units = down_w.shape[0]
    gate_pre, up_pre = preact[:, :hidden_units], preact[:, hidden_units:]
    sig = jax.nn.sigmoid(gate_pre)
    hidden_shard = (gate_pre * sig * up_pre).astype(BF)
    hidden_half, hidden = gather_rows(hidden_shard, y_pos, core, chips)

    returned = exchange(dot(hidden, down_w).astype(BF))

    arrived_grad = tie(arrived_grad, hidden_shard)
    hid_far = core_swap(dot(rows_at(arrived_grad, 1 - core, half_rows), down_w, 1, 1).astype(BF))
    hid_own = dot(rows_at(arrived_grad, core, half_rows), down_w, 1, 1).astype(BF)
    hid_far = tie(hid_far, hidden_half)
    hidden_grad = scatter_sum(pieces_of(hid_own, hid_far, y_pos, chips))
    gate_grad = hidden_grad * up_pre * sig * (1.0 + gate_pre * (1.0 - sig))
    up_grad = hidden_grad * gate_pre * sig
    pre_shard = jnp.concatenate([gate_grad, up_grad], axis=1).astype(BF)
    _, pre_grad = gather_rows(pre_shard, y_pos, core, chips)
    returned_grad = exchange(dot(pre_grad, gate_up, 1, 1).astype(BF))

    weight_grad = dot(hidden, arrived_grad, 0, 0)
    far_grad = expert_swap(weight_grad.astype(BF))
    one = jnp.where(own_swap, far_one.astype(F32), first_moment[0])
    two = jnp.where(own_swap, far_two.astype(F32), second_moment[0])
    grad = jnp.where(own_swap, far_grad.astype(F32), weight_grad)
    new_one = beta_first * one + (1.0 - beta_first) * grad
    new_two = beta_second * two + (1.0 - beta_second) * grad * grad
    step_dir = (new_one / (jnp.sqrt(new_two) + adam_eps)).astype(BF)

    match = token_ids[:, None] == masked_route[None, :]
    top = lax.reduce_precision(weighted, 8, 7)
    rest = weighted - top
    mixed = (
        dot(jnp.where(match, top[None, :], 0.0).astype(BF), returned)
        + dot(jnp.where(match, rest[None, :], 0.0).astype(BF), returned)
    ).astype(BF)
    token_grad = dot(match.astype(BF), returned_grad).astype(BF)
    return (mixed, token_grad, new_one[None], new_two[None], step_dir[None])


def solution(mesh):
    return jax.shard_map(
        shards,
        mesh=mesh,
        in_specs=(
            P("expert", "dp"),
            P("expert", "dp"),
            P("expert", None, None),
            P("expert", None),
            P("expert", None, None),
            P(),
            P("expert", "dp", None),
            P("expert", "dp", None),
            P("expert", None, "dp"),
            P("expert", None, "dp"),
            P("expert", None, "dp"),
        ),
        out_specs=(
            P("expert", "dp"),
            P("expert", "dp"),
            P("expert", None, "dp"),
            P("expert", None, "dp"),
            P("expert", None, "dp"),
        ),
        check_vma=False,
    )
```

```python
import jax
import jax.numpy as jnp
from jax import lax
from jax.sharding import PartitionSpec as P


beta_first = 0.9
beta_second = 0.999
adam_eps = 1e-08
BF = jnp.bfloat16
F32 = jnp.float32


def dot(a, b, ca=1, cb=0):
    return lax.dot_general(a, b, (((ca,), (cb,)), ((), ())), preferred_element_type=F32)


def core_swap(block):
    return lax.ppermute(block, "dp", [(i, i ^ 1) for i in range(lax.axis_size("dp"))])


def chip_shift(block, step):
    count = lax.axis_size("dp")
    return lax.ppermute(block, "dp", [(i, (i + 2 * step) % count) for i in range(count)])


def expert_swap(block):
    count = lax.axis_size("expert")
    return lax.ppermute(block, "expert", [(i, i ^ (count // 2)) for i in range(count)])


def rows_at(block, index, rows):
    return lax.dynamic_slice_in_dim(block, index * rows, rows, 0)


def tie(value, *others):
    return lax.optimization_barrier((value,) + others)[0]


def scatter_sum(partial, y_pos, chips):
    rows = partial.shape[0] // chips
    total = rows_at(partial, y_pos, rows).astype(F32)
    for step in (2, 1, 3):
        piece = rows_at(partial, (y_pos + step) % chips, rows)
        came = chip_shift(piece, step)
        total = total + came.astype(F32)
    return total


def gather_rows(shard, y_pos, chips):
    rows = shard.shape[0]
    full = jnp.zeros((chips * rows,) + shard.shape[1:], shard.dtype)
    full = lax.dynamic_update_slice_in_dim(full, shard, y_pos * rows, 0)
    for step in (1, 3, 2):
        piece = chip_shift(shard, step)
        full = lax.dynamic_update_slice_in_dim(full, piece, ((y_pos - step) % chips) * rows, 0)
    return full


def pair_rows(block):
    far = core_swap(block)
    return jnp.concatenate([block, far], axis=0)


def pair_sum(partial):
    split = partial.shape[0] // 2
    far = core_swap(partial[split:].astype(BF))
    return partial[:split] + far.astype(F32)


def shards(
    tokens,
    cotangent,
    slot_tokens,
    slot_counts,
    slot_gates,
    swap_pairs,
    gate_weight,
    up_weight,
    down_weight,
    first_moment,
    second_moment,
):
    tok_count, model_cols = tokens.shape
    experts = slot_counts.shape[1]
    capacity = slot_tokens.shape[2]
    own_slots = capacity // 2
    rows = experts * own_slots
    pair_cols = 2 * model_cols
    chips = lax.axis_size("dp") // 2
    dp_pos = lax.axis_index("dp")
    core, y_pos = dp_pos % 2, dp_pos // 2
    position = lax.axis_index("expert")
    half_count = swap_pairs.shape[0]
    own_swap = (
        jnp.sum(jnp.where(jnp.arange(half_count) == position % half_count, swap_pairs, 0)) > 0
    )

    def own_part(table):
        return lax.dynamic_slice_in_dim(table, core * own_slots, own_slots, 1)

    live = (own_part(jnp.arange(capacity)[None, :]) < slot_counts[0][:, None]).reshape(-1)
    route = own_part(slot_tokens[0]).reshape(-1)
    weighted = jnp.where(live, own_part(slot_gates[0]).reshape(-1), 0.0)
    masked_route = jnp.where(live, route, -1)
    token_ids = jnp.arange(tok_count)

    def exchange(block):
        return lax.all_to_all(
            block.reshape(experts, own_slots, pair_cols), "expert", 0, 0, tiled=True
        ).reshape(rows, pair_cols)

    token_cols = pair_rows(tokens.T)
    pick = (masked_route[:, None] == token_ids[None, :]).astype(BF)
    arrived = exchange(dot(pick, token_cols, 1, 1).astype(BF))
    grad_cols = pair_rows(cotangent.T)
    grad_rows = (dot(pick, grad_cols, 1, 1) * weighted[:, None]).astype(BF)
    gate_up = jnp.concatenate([pair_rows(gate_weight[0]), pair_rows(up_weight[0])], axis=1)
    down_cols = pair_rows(down_weight[0].T)
    moment_one = first_moment[0].T
    moment_two = second_moment[0].T
    gate_up, down_cols, grad_rows, arrived = lax.optimization_barrier(
        (gate_up, down_cols, grad_rows, arrived)
    )
    arrived_grad = exchange(grad_rows)
    far_one = expert_swap(moment_one.astype(BF))
    far_two = expert_swap(moment_two.astype(BF))

    preact = scatter_sum(dot(arrived, gate_up).astype(BF), y_pos, chips)
    hidden_units = down_weight.shape[1]
    gate_pre, up_pre = preact[:, :hidden_units], preact[:, hidden_units:]
    sig = jax.nn.sigmoid(gate_pre)
    hidden_shard = (gate_pre * sig * up_pre).astype(BF)
    hidden = gather_rows(hidden_shard, y_pos, chips)
    returned = exchange(dot(hidden, down_cols, 1, 1).astype(BF))

    arrived_grad = tie(arrived_grad, hidden_shard)
    hidden_part = tie(dot(arrived_grad, down_cols).astype(BF), hidden)
    hidden_grad = scatter_sum(hidden_part, y_pos, chips)
    gate_grad = hidden_grad * up_pre * sig * (1.0 + gate_pre * (1.0 - sig))
    up_grad = hidden_grad * gate_pre * sig
    pre_shard = jnp.concatenate([gate_grad, up_grad], axis=1).astype(BF)
    pre_grad = gather_rows(pre_shard, y_pos, chips)
    returned_grad = exchange(dot(pre_grad, gate_up, 1, 1).astype(BF))

    weight_grad = pair_sum(dot(tie(arrived_grad, pre_shard), hidden, 0, 0))
    far_grad = expert_swap(weight_grad.astype(BF))
    one = jnp.where(own_swap, far_one.astype(F32), moment_one)
    two = jnp.where(own_swap, far_two.astype(F32), moment_two)
    grad = jnp.where(own_swap, far_grad.astype(F32), weight_grad)
    new_one = beta_first * one + (1.0 - beta_first) * grad
    new_two = beta_second * two + (1.0 - beta_second) * grad * grad
    step_dir = (new_one / (jnp.sqrt(new_two) + adam_eps)).astype(BF)

    match = masked_route[:, None] == token_ids[None, :]
    top = lax.reduce_precision(weighted, 8, 7)
    rest = weighted - top
    mixed = pair_sum(
        dot(returned, jnp.where(match, top[:, None], 0.0).astype(BF), 0, 0)
        + dot(returned, jnp.where(match, rest[:, None], 0.0).astype(BF), 0, 0),
    ).astype(BF)
    returned_grad = tie(returned_grad, mixed, step_dir)
    token_grad = pair_sum(dot(returned_grad, match.astype(BF), 0, 0)).astype(BF)
    return (mixed.T, token_grad.T, new_one.T[None], new_two.T[None], step_dir.T[None])


def solution(mesh):
    return jax.shard_map(
        shards,
        mesh=mesh,
        in_specs=(
            P("expert", "dp"),
            P("expert", "dp"),
            P("expert", None, None),
            P("expert", None),
            P("expert", None, None),
            P(),
            P("expert", "dp", None),
            P("expert", "dp", None),
            P("expert", None, "dp"),
            P("expert", None, "dp"),
            P("expert", None, "dp"),
        ),
        out_specs=(
            P("expert", "dp"),
            P("expert", "dp"),
            P("expert", None, "dp"),
            P("expert", None, "dp"),
            P("expert", None, "dp"),
        ),
        check_vma=False,
    )
```

```python
import jax
import jax.numpy as jnp
from jax import lax
from jax.experimental import pallas as pl
from jax.experimental.pallas import tpu as pltpu
from jax.sharding import PartitionSpec as P


beta_first = 0.9
beta_second = 0.999
adam_eps = 1e-08
BF = jnp.bfloat16
F32 = jnp.float32


def dot(a, b, ca=1, cb=0):
    return lax.dot_general(a, b, (((ca,), (cb,)), ((), ())), preferred_element_type=F32)


def core_swap(block):
    return lax.ppermute(block, "dp", [(i, i ^ 1) for i in range(lax.axis_size("dp"))])


def chip_shift(block, step):
    count = lax.axis_size("dp")
    return lax.ppermute(block, "dp", [(i, (i + 2 * step) % count) for i in range(count)])


def expert_swap(block):
    count = lax.axis_size("expert")
    return lax.ppermute(block, "expert", [(i, i ^ (count // 2)) for i in range(count)])


def rows_at(block, index, rows):
    return lax.dynamic_slice_in_dim(block, index * rows, rows, 0)


def tie(value, *others):
    return lax.optimization_barrier((value,) + others)[0]


def tie_all(values, *others):
    return lax.optimization_barrier(tuple(values) + others)[: len(values)]


def scatter_sum(partial, y_pos, chips):
    rows = partial.shape[0] // chips
    total = rows_at(partial, y_pos, rows).astype(F32)
    for step in (2, 1, 3):
        piece = rows_at(partial, (y_pos + step) % chips, rows)
        came = chip_shift(piece, step)
        total = total + came.astype(F32)
    return total


def gather_rows(shard, y_pos, chips, after=()):
    rows = shard.shape[0]
    full = jnp.broadcast_to(shard[None], (chips,) + shard.shape).reshape(-1, shard.shape[1])
    pieces = []
    for step in (1, 3, 2):
        piece = chip_shift(shard, step)
        pieces.append((step, piece))
    held = tie_all([piece for _, piece in pieces], *after)
    for (step, _), piece in zip(pieces, held):
        full = lax.dynamic_update_slice_in_dim(full, piece, ((y_pos - step) % chips) * rows, 0)
    return full


def pair_rows(block):
    far = core_swap(block)
    return jnp.concatenate([block, far], axis=0)


def join_weights(gate_own, up_own, gate_far, up_far):
    rows, units = gate_own.shape
    steps = 4
    block = rows // steps

    def body(gate_a, up_a, gate_b, up_b, out):
        first = pl.program_id(0) < steps

        @pl.when(first)
        def _():
            out[:, :units] = gate_a[...]
            out[:, units:] = up_a[...]

        @pl.when(jnp.logical_not(first))
        def _():
            out[:, :units] = gate_b[...]
            out[:, units:] = up_b[...]

    near = pl.BlockSpec((block, units), lambda i: (jnp.minimum(i, steps - 1), 0))
    far = pl.BlockSpec((block, units), lambda i: (jnp.maximum(i - steps, 0), 0))
    moved = 8 * rows * units
    return pl.pallas_call(
        body,
        out_shape=jax.ShapeDtypeStruct((2 * rows, 2 * units), gate_own.dtype),
        grid=(2 * steps,),
        in_specs=[near, near, far, far],
        out_specs=pl.BlockSpec((block, 2 * units), lambda i: (i, 0)),
        compiler_params=pltpu.CompilerParams(vmem_limit_bytes=8 << 20),
        cost_estimate=pl.CostEstimate(flops=0, bytes_accessed=2 * moved, transcendentals=0),
    )(gate_own, up_own, gate_far, up_far)


def pair_sum(partial):
    split = partial.shape[0] // 2
    far = core_swap(partial[split:].astype(BF))
    return partial[:split] + far.astype(F32)


def shards(
    tokens,
    cotangent,
    slot_tokens,
    slot_counts,
    slot_gates,
    swap_pairs,
    gate_weight,
    up_weight,
    down_weight,
    first_moment,
    second_moment,
):
    tok_count, model_cols = tokens.shape
    experts = slot_counts.shape[1]
    capacity = slot_tokens.shape[2]
    own_slots = capacity // 2
    pair_cols = 2 * model_cols
    chips = lax.axis_size("dp") // 2
    dp_pos = lax.axis_index("dp")
    core, y_pos = dp_pos % 2, dp_pos // 2
    position = lax.axis_index("expert")
    half_count = swap_pairs.shape[0]
    own_swap = (
        jnp.sum(jnp.where(jnp.arange(half_count) == position % half_count, swap_pairs, 0)) > 0
    )

    def own_part(table):
        return lax.dynamic_slice_in_dim(table, core * own_slots, own_slots, 1)

    live = (own_part(jnp.arange(capacity)[None, :]) < slot_counts[0][:, None]).reshape(-1)
    route = own_part(slot_tokens[0]).reshape(-1)
    weighted = jnp.where(live, own_part(slot_gates[0]).reshape(-1), 0.0)
    masked_route = jnp.where(live, route, -1)
    token_ids = jnp.arange(tok_count)

    def exchange(block, slots):
        return lax.all_to_all(
            block.reshape(experts, slots, pair_cols), "expert", 0, 0, tiled=True
        ).reshape(experts * slots, pair_cols)

    token_cols = pair_rows(tokens.T)
    part_slots = own_slots // 2
    blocks = []
    for part in range(2):
        ids = masked_route.reshape(experts, own_slots)[:, part * part_slots :][:, :part_slots]
        picked = (ids.reshape(-1)[:, None] == token_ids[None, :]).astype(BF)
        blocks.append(dot(picked, token_cols, 1, 1).astype(BF))
    pick = (masked_route[:, None] == token_ids[None, :]).astype(BF)
    grad_cols = pair_rows(cotangent.T)
    grad_rows = (dot(pick, grad_cols, 1, 1) * weighted[:, None]).astype(BF)
    far_gate = core_swap(gate_weight[0])
    far_up = core_swap(up_weight[0])
    gate_up = join_weights(gate_weight[0], up_weight[0], far_gate, far_up)
    down_cols = pair_rows(down_weight[0].T)
    arrived = [exchange(blocks[0], part_slots)]
    later, gate_up, down_cols, grad_rows = lax.optimization_barrier(
        (blocks[1], gate_up, down_cols, grad_rows)
    )
    arrived.append(exchange(later, part_slots))
    moment_one = first_moment[0].T
    moment_two = second_moment[0].T
    arrived_grad = exchange(grad_rows, own_slots)
    far_one = expert_swap(tie(moment_one, arrived[0]).astype(BF))
    far_two = expert_swap(tie(moment_two, arrived[0]).astype(BF))

    hidden_units = down_weight.shape[1]
    groups = experts // chips

    def merge(parts):
        split = [part.reshape(groups, 1, part_slots, -1) for part in parts]
        return jnp.concatenate(split, axis=1).reshape(groups * own_slots, -1)

    gates, hidden_parts = [], []
    for x in arrived:
        preact = scatter_sum(dot(x, gate_up).astype(BF), y_pos, chips)
        gate_pre, up_pre = preact[:, :hidden_units], preact[:, hidden_units:]
        sig = jax.nn.sigmoid(gate_pre)
        gates.append((gate_pre, up_pre, sig))
        hidden_parts.append((gate_pre * sig * up_pre).astype(BF))
    hidden_shard = merge(hidden_parts)
    arrived_grad = tie(arrived_grad, hidden_shard)
    hidden_part = dot(arrived_grad, down_cols).astype(BF)
    hidden = gather_rows(hidden_shard, y_pos, chips, (hidden_part,))
    returned = exchange(dot(hidden, down_cols, 1, 1).astype(BF), own_slots)

    hidden_part = tie(hidden_part, hidden)
    hidden_grad = scatter_sum(hidden_part, y_pos, chips)
    grad_parts = []
    for part, (gate_pre, up_pre, sig) in enumerate(gates):
        grad = hidden_grad.reshape(groups, 2, part_slots, hidden_units)[:, part]
        grad = grad.reshape(-1, hidden_units)
        gate_grad = grad * up_pre * sig * (1.0 + gate_pre * (1.0 - sig))
        up_grad = grad * gate_pre * sig
        grad_parts.append(jnp.concatenate([gate_grad, up_grad], axis=1).astype(BF))
    pre_shard = merge(grad_parts)
    weight_grad = pair_sum(dot(tie(arrived_grad, pre_shard), hidden, 0, 0))
    sent_grad = weight_grad.astype(BF)
    far_grad = expert_swap(sent_grad)
    pre_grad = gather_rows(pre_shard, y_pos, chips, (sent_grad,))
    returned_grad = exchange(dot(pre_grad, gate_up, 1, 1).astype(BF), own_slots)

    one = jnp.where(own_swap, far_one.astype(F32), moment_one)
    two = jnp.where(own_swap, far_two.astype(F32), moment_two)
    grad = jnp.where(own_swap, far_grad.astype(F32), weight_grad)
    new_one = beta_first * one + (1.0 - beta_first) * grad
    new_two = beta_second * two + (1.0 - beta_second) * grad * grad
    step_dir = (new_one / (jnp.sqrt(new_two) + adam_eps)).astype(BF)

    match = masked_route[:, None] == token_ids[None, :]
    top = lax.reduce_precision(weighted, 8, 7)
    rest = weighted - top
    mixed = pair_sum(
        dot(returned, jnp.where(match, top[:, None], 0.0).astype(BF), 0, 0)
        + dot(returned, jnp.where(match, rest[:, None], 0.0).astype(BF), 0, 0),
    ).astype(BF)
    returned_grad = tie(returned_grad, mixed, step_dir)
    token_grad = pair_sum(dot(returned_grad, match.astype(BF), 0, 0)).astype(BF)
    return (mixed.T, token_grad.T, new_one.T[None], new_two.T[None], step_dir.T[None])


def solution(mesh):
    return jax.shard_map(
        shards,
        mesh=mesh,
        in_specs=(
            P("expert", "dp"),
            P("expert", "dp"),
            P("expert", None, None),
            P("expert", None),
            P("expert", None, None),
            P(),
            P("expert", "dp", None),
            P("expert", "dp", None),
            P("expert", None, "dp"),
            P("expert", None, "dp"),
            P("expert", None, "dp"),
        ),
        out_specs=(
            P("expert", "dp"),
            P("expert", "dp"),
            P("expert", None, "dp"),
            P("expert", None, "dp"),
            P("expert", None, "dp"),
        ),
        check_vma=False,
    )
```

```python
import jax
import jax.numpy as jnp
from jax import lax
from jax.experimental import pallas as pl
from jax.experimental.pallas import tpu as pltpu
from jax.sharding import PartitionSpec as P


beta_first = 0.9
beta_second = 0.999
adam_eps = 1e-08
BF = jnp.bfloat16
F32 = jnp.float32


def dot(a, b, ca=1, cb=0):
    return lax.dot_general(a, b, (((ca,), (cb,)), ((), ())), preferred_element_type=F32)


def core_swap(block):
    return lax.ppermute(block, "dp", [(i, i ^ 1) for i in range(lax.axis_size("dp"))])


def chip_shift(block, step):
    count = lax.axis_size("dp")
    return lax.ppermute(block, "dp", [(i, (i + 2 * step) % count) for i in range(count)])


def expert_swap(block):
    count = lax.axis_size("expert")
    return lax.ppermute(block, "expert", [(i, i ^ (count // 2)) for i in range(count)])


def rows_at(block, index, rows):
    return lax.dynamic_slice_in_dim(block, index * rows, rows, 0)


def tie(value, *others):
    return lax.optimization_barrier((value,) + others)[0]


def tie_all(values, *others):
    return lax.optimization_barrier(tuple(values) + others)[: len(values)]


def scatter_sum(partial, y_pos, chips):
    rows = partial.shape[0] // chips
    total = rows_at(partial, y_pos, rows).astype(F32)
    for step in (2, 1, 3):
        piece = rows_at(partial, (y_pos + step) % chips, rows)
        came = chip_shift(piece, step)
        total = total + came.astype(F32)
    return total


def ring_sum(partial, y_pos, chips):
    rows = partial.shape[0] // (2 * chips)

    def half(step, part):
        return rows_at(partial, 2 * ((y_pos + step) % chips) + part, rows)

    from_left = chip_shift(jnp.concatenate([half(2, 0), half(1, 1)]), 1)
    from_right = chip_shift(jnp.concatenate([half(2, 1), half(3, 0)]), chips - 1)
    on_right = (half(1, 0).astype(F32) + from_left[:rows].astype(F32)).astype(BF)
    on_left = (half(3, 1).astype(F32) + from_right[:rows].astype(F32)).astype(BF)
    on_right, on_left = lax.optimization_barrier((on_right, on_left))
    far_left = chip_shift(on_right, 1)
    far_right = chip_shift(on_left, chips - 1)
    top = half(0, 0).astype(F32) + from_right[rows:].astype(F32) + far_left.astype(F32)
    low = half(0, 1).astype(F32) + from_left[rows:].astype(F32) + far_right.astype(F32)
    return jnp.concatenate([top, low])


def ring_gather(shard, y_pos, chips, after=()):
    rows = shard.shape[0]
    mid = rows // 2
    left = chip_shift(shard, 1)
    right = chip_shift(shard, chips - 1)
    far_top = chip_shift(left[:mid], 1)
    far_low = chip_shift(right[mid:], chips - 1)
    full = jnp.broadcast_to(shard[None], (chips,) + shard.shape).reshape(-1, shard.shape[1])
    pieces = tie_all([left, right, far_top, far_low], *after)
    spots = ((3, 0), (1, 0), (2, 0), (2, mid))
    for (step, offset), piece in zip(spots, pieces):
        at = ((y_pos + step) % chips) * rows + offset
        full = lax.dynamic_update_slice_in_dim(full, piece, at, 0)
    return full


def pair_rows(block):
    far = core_swap(block)
    return jnp.concatenate([block, far], axis=0)


def join_weights(gate_own, up_own, gate_far, up_far):
    rows, units = gate_own.shape
    steps = 4
    block = rows // steps

    def body(gate_a, up_a, gate_b, up_b, out):
        first = pl.program_id(0) < steps

        @pl.when(first)
        def _():
            out[:, :units] = gate_a[...]
            out[:, units:] = up_a[...]

        @pl.when(jnp.logical_not(first))
        def _():
            out[:, :units] = gate_b[...]
            out[:, units:] = up_b[...]

    near = pl.BlockSpec((block, units), lambda i: (jnp.minimum(i, steps - 1), 0))
    far = pl.BlockSpec((block, units), lambda i: (jnp.maximum(i - steps, 0), 0))
    moved = 8 * rows * units
    return pl.pallas_call(
        body,
        out_shape=jax.ShapeDtypeStruct((2 * rows, 2 * units), gate_own.dtype),
        grid=(2 * steps,),
        in_specs=[near, near, far, far],
        out_specs=pl.BlockSpec((block, 2 * units), lambda i: (i, 0)),
        compiler_params=pltpu.CompilerParams(vmem_limit_bytes=8 << 20),
        cost_estimate=pl.CostEstimate(flops=0, bytes_accessed=2 * moved, transcendentals=0),
    )(gate_own, up_own, gate_far, up_far)


def pair_sum(partial):
    split = partial.shape[0] // 2
    far = core_swap(partial[split:].astype(BF))
    return partial[:split] + far.astype(F32)


def shards(
    tokens,
    cotangent,
    slot_tokens,
    slot_counts,
    slot_gates,
    swap_pairs,
    gate_weight,
    up_weight,
    down_weight,
    first_moment,
    second_moment,
):
    tok_count, model_cols = tokens.shape
    experts = slot_counts.shape[1]
    capacity = slot_tokens.shape[2]
    own_slots = capacity // 2
    rows = experts * own_slots
    pair_cols = 2 * model_cols
    chips = lax.axis_size("dp") // 2
    dp_pos = lax.axis_index("dp")
    core, y_pos = dp_pos % 2, dp_pos // 2
    position = lax.axis_index("expert")
    half_count = swap_pairs.shape[0]
    own_swap = (
        jnp.sum(jnp.where(jnp.arange(half_count) == position % half_count, swap_pairs, 0)) > 0
    )

    def own_part(table):
        return lax.dynamic_slice_in_dim(table, core * own_slots, own_slots, 1)

    live = (own_part(jnp.arange(capacity)[None, :]) < slot_counts[0][:, None]).reshape(-1)
    route = own_part(slot_tokens[0]).reshape(-1)
    weighted = jnp.where(live, own_part(slot_gates[0]).reshape(-1), 0.0)
    masked_route = jnp.where(live, route, -1)
    token_ids = jnp.arange(tok_count)

    def exchange(block):
        return lax.all_to_all(
            block.reshape(experts, own_slots, pair_cols), "expert", 0, 0, tiled=True
        ).reshape(rows, pair_cols)

    token_cols = pair_rows(tokens.T)
    pick = (masked_route[:, None] == token_ids[None, :]).astype(BF)
    arrived = exchange(dot(pick, token_cols, 1, 1).astype(BF))
    grad_cols = pair_rows(cotangent.T)
    grad_rows = (dot(pick, grad_cols, 1, 1) * weighted[:, None]).astype(BF)
    far_gate = core_swap(gate_weight[0])
    far_up = core_swap(up_weight[0])
    gate_up = join_weights(gate_weight[0], up_weight[0], far_gate, far_up)
    down_cols = pair_rows(down_weight[0].T)
    arrived, gate_up, down_cols, grad_rows = lax.optimization_barrier(
        (arrived, gate_up, down_cols, grad_rows)
    )
    moment_one = first_moment[0].T
    moment_two = second_moment[0].T
    arrived_grad = exchange(grad_rows)
    far_one = expert_swap(tie(moment_one, arrived).astype(BF))
    far_two = expert_swap(tie(moment_two, arrived).astype(BF))

    hidden_units = down_weight.shape[1]
    preact = ring_sum(dot(arrived, gate_up).astype(BF), y_pos, chips)
    gate_pre, up_pre = preact[:, :hidden_units], preact[:, hidden_units:]
    sig = jax.nn.sigmoid(gate_pre)
    hidden_shard = (gate_pre * sig * up_pre).astype(BF)
    hidden = ring_gather(hidden_shard, y_pos, chips)
    out_rows, arrived_grad = lax.optimization_barrier(
        (dot(hidden, down_cols, 1, 1).astype(BF), arrived_grad)
    )
    returned = exchange(out_rows)

    hidden_part = dot(arrived_grad, down_cols).astype(BF)
    hidden_grad = scatter_sum(hidden_part, y_pos, chips)
    gate_grad = hidden_grad * up_pre * sig * (1.0 + gate_pre * (1.0 - sig))
    up_grad = hidden_grad * gate_pre * sig
    pre_shard = jnp.concatenate([gate_grad, up_grad], axis=1).astype(BF)
    weight_grad = pair_sum(dot(tie(arrived_grad, pre_shard), hidden, 0, 0))
    sent_grad = weight_grad.astype(BF)
    far_grad = expert_swap(sent_grad)
    pre_grad = ring_gather(pre_shard, y_pos, chips, (sent_grad,))
    returned_grad = exchange(dot(pre_grad, gate_up, 1, 1).astype(BF))

    one = jnp.where(own_swap, far_one.astype(F32), moment_one)
    two = jnp.where(own_swap, far_two.astype(F32), moment_two)
    grad = jnp.where(own_swap, far_grad.astype(F32), weight_grad)
    new_one = beta_first * one + (1.0 - beta_first) * grad
    new_two = beta_second * two + (1.0 - beta_second) * grad * grad
    step_dir = (new_one / (jnp.sqrt(new_two) + adam_eps)).astype(BF)

    match = masked_route[:, None] == token_ids[None, :]
    top = lax.reduce_precision(weighted, 8, 7)
    rest = weighted - top
    mixed = pair_sum(
        dot(returned, jnp.where(match, top[:, None], 0.0).astype(BF), 0, 0)
        + dot(returned, jnp.where(match, rest[:, None], 0.0).astype(BF), 0, 0),
    ).astype(BF)
    returned_grad = tie(returned_grad, mixed, step_dir)
    token_grad = pair_sum(dot(returned_grad, match.astype(BF), 0, 0)).astype(BF)
    return (mixed.T, token_grad.T, new_one.T[None], new_two.T[None], step_dir.T[None])


def solution(mesh):
    return jax.shard_map(
        shards,
        mesh=mesh,
        in_specs=(
            P("expert", "dp"),
            P("expert", "dp"),
            P("expert", None, None),
            P("expert", None),
            P("expert", None, None),
            P(),
            P("expert", "dp", None),
            P("expert", "dp", None),
            P("expert", None, "dp"),
            P("expert", None, "dp"),
            P("expert", None, "dp"),
        ),
        out_specs=(
            P("expert", "dp"),
            P("expert", "dp"),
            P("expert", None, "dp"),
            P("expert", None, "dp"),
            P("expert", None, "dp"),
        ),
        check_vma=False,
    )
```

```python
import jax
import jax.numpy as jnp
from jax import lax
from jax.experimental import pallas as pl
from jax.experimental.pallas import tpu as pltpu
from jax.sharding import PartitionSpec as P


beta_first = 0.9
beta_second = 0.999
adam_eps = 1e-08
BF = jnp.bfloat16
F32 = jnp.float32


def dot(a, b, ca=1, cb=0):
    return lax.dot_general(a, b, (((ca,), (cb,)), ((), ())), preferred_element_type=F32)


def core_swap(block):
    return lax.ppermute(block, "dp", [(i, i ^ 1) for i in range(lax.axis_size("dp"))])


def chip_shift(block, step):
    count = lax.axis_size("dp")
    return lax.ppermute(block, "dp", [(i, (i + 2 * step) % count) for i in range(count)])


def expert_swap(block):
    count = lax.axis_size("expert")
    return lax.ppermute(block, "expert", [(i, i ^ (count // 2)) for i in range(count)])


def tie(value, *others):
    return lax.optimization_barrier((value,) + others)[0]


def tie_all(values, *others):
    return lax.optimization_barrier(tuple(values) + others)[: len(values)]


def ordered_dot(y_pos, left, right, units, sizes):
    rows, depth = left.shape
    width = right.shape[1]
    unit = rows // len(units)
    per_block = len(units) // 4
    tile = 512

    def body(pos, left_ref, right_ref, *refs):
        outs, ordered = refs[:-1], refs[-1]

        @pl.when(pl.program_id(0) == 0)
        def _():
            for place, (step, part) in enumerate(units):
                at = (lax.rem(pos[0] + step, 4) * per_block + part) * unit
                ordered[place * unit : (place + 1) * unit, :] = left_ref[
                    pl.ds(pl.multiple_of(at, unit), unit), :
                ]

        start = 0
        for out in outs:
            size = out.shape[0]
            out[...] = dot(ordered[start : start + size, :], right_ref[...]).astype(BF)
            start += size

    return pl.pallas_call(
        body,
        out_shape=[pltpu.HBM((size, width), BF) for size in sizes],
        grid_spec=pltpu.PrefetchScalarGridSpec(
            num_scalar_prefetch=1,
            grid=(width // tile,),
            in_specs=[
                pl.BlockSpec((rows, depth), lambda i, pos: (0, 0)),
                pl.BlockSpec((depth, tile), lambda i, pos: (0, i)),
            ],
            out_specs=[pl.BlockSpec((size, tile), lambda i, pos: (0, i)) for size in sizes],
            scratch_shapes=[pltpu.VMEM((rows, depth), BF)],
        ),
        compiler_params=pltpu.CompilerParams(vmem_limit_bytes=16 << 20),
        cost_estimate=pl.CostEstimate(
            flops=2 * rows * depth * width,
            bytes_accessed=2 * (rows * depth + depth * width + rows * width),
            transcendentals=0,
        ),
    )(y_pos.reshape(1), left, pltpu.with_memory_space_constraint(right, pltpu.HBM))


def gathered_dot(y_pos, parts, right, keep):
    own, _, _, _, _ = parts
    rows, depth = own.shape
    width = right.shape[0]
    total = 4 * rows
    mid = rows // 2
    tile = 512
    steps = depth // tile

    def body(pos, own_ref, left_ref, right_ref, top_ref, low_ref, w_ref, out, *refs):
        full, acc = refs[-2:]
        k = pl.program_id(0)

        @pl.when(k == 0)
        def _():
            for step, offset, ref in (
                (0, 0, own_ref),
                (3, 0, left_ref),
                (1, 0, right_ref),
                (2, 0, top_ref),
                (2, mid, low_ref),
            ):
                at = lax.rem(pos[0] + step, 4) * rows + offset
                size = ref.shape[0]
                if keep:
                    refs[0][pl.ds(pl.multiple_of(at, mid), size), :] = ref[...]
                for t in range(steps):
                    full[t, pl.ds(pl.multiple_of(at, mid), size), :] = ref[
                        :, t * tile : (t + 1) * tile
                    ]

        term = dot(full[k], w_ref[...], 1, 1)

        @pl.when(k == 0)
        def _():
            acc[...] = term

        @pl.when(jnp.logical_and(k > 0, k < steps - 1))
        def _():
            acc[...] += term

        @pl.when(k == steps - 1)
        def _():
            out[...] = (acc[...] + term).astype(BF)

    def whole(shape):
        return pl.BlockSpec(shape, lambda k, pos: (0,) * len(shape))

    out_shape = [pltpu.HBM((total, width), BF)]
    out_specs = [whole((total, width))]
    if keep:
        out_shape.append(pltpu.HBM((total, depth), BF))
        out_specs.append(whole((total, depth)))
    scratch = [pltpu.VMEM((steps, total, tile), BF), pltpu.VMEM((total, width), F32)]
    return pl.pallas_call(
        body,
        out_shape=out_shape,
        grid_spec=pltpu.PrefetchScalarGridSpec(
            num_scalar_prefetch=1,
            grid=(steps,),
            in_specs=[whole(part.shape) for part in parts]
            + [pl.BlockSpec((width, tile), lambda k, pos: (0, k))],
            out_specs=out_specs,
            scratch_shapes=scratch,
        ),
        compiler_params=pltpu.CompilerParams(vmem_limit_bytes=24 << 20),
        cost_estimate=pl.CostEstimate(
            flops=2 * total * depth * width,
            bytes_accessed=2 * (total * depth + depth * width + total * width),
            transcendentals=0,
        ),
    )(y_pos.reshape(1), *parts, pltpu.with_memory_space_constraint(right, pltpu.HBM))


RING_UNITS = ((2, 0), (1, 1), (2, 1), (3, 0), (0, 0), (0, 1), (1, 0), (3, 1))


def ring_sum(to_right, to_left, rest, chips):
    rows = rest.shape[0] // 4
    own_top, own_low, pass_right, pass_left = (rest[i * rows :][:rows] for i in range(4))
    from_left = chip_shift(to_right, 1)
    from_right = chip_shift(to_left, chips - 1)
    on_right = (pass_right.astype(F32) + from_left[:rows].astype(F32)).astype(BF)
    on_left = (pass_left.astype(F32) + from_right[:rows].astype(F32)).astype(BF)
    on_right, on_left = lax.optimization_barrier((on_right, on_left))
    far_left = chip_shift(on_right, 1)
    far_right = chip_shift(on_left, chips - 1)
    top = own_top.astype(F32) + from_right[rows:].astype(F32) + far_left.astype(F32)
    low = own_low.astype(F32) + from_left[rows:].astype(F32) + far_right.astype(F32)
    return jnp.concatenate([top, low])


def ring_gather(shard, chips):
    mid = shard.shape[0] // 2
    left = chip_shift(shard, 1)
    right = chip_shift(shard, chips - 1)
    far_top = chip_shift(left[:mid], 1)
    far_low = chip_shift(right[mid:], chips - 1)
    return shard, left, right, far_top, far_low


def pair_rows(block):
    far = core_swap(block)
    return jnp.concatenate([block, far], axis=0)


def join_weights(gate_own, up_own, gate_far, up_far):
    rows, units = gate_own.shape
    steps = 4
    block = rows // steps

    def body(gate_a, up_a, gate_b, up_b, out):
        first = pl.program_id(0) < steps

        @pl.when(first)
        def _():
            out[:, :units] = gate_a[...]
            out[:, units:] = up_a[...]

        @pl.when(jnp.logical_not(first))
        def _():
            out[:, :units] = gate_b[...]
            out[:, units:] = up_b[...]

    near = pl.BlockSpec((block, units), lambda i: (jnp.minimum(i, steps - 1), 0))
    far = pl.BlockSpec((block, units), lambda i: (jnp.maximum(i - steps, 0), 0))
    moved = 8 * rows * units
    return pl.pallas_call(
        body,
        out_shape=pltpu.HBM((2 * rows, 2 * units), gate_own.dtype),
        grid=(2 * steps,),
        in_specs=[near, near, far, far],
        out_specs=pl.BlockSpec((block, 2 * units), lambda i: (i, 0)),
        compiler_params=pltpu.CompilerParams(vmem_limit_bytes=8 << 20),
        cost_estimate=pl.CostEstimate(flops=0, bytes_accessed=2 * moved, transcendentals=0),
    )(gate_own, up_own, gate_far, up_far)


def pair_sum(partial):
    split = partial.shape[0] // 2
    far = core_swap(partial[split:].astype(BF))
    return partial[:split] + far.astype(F32)


def shards(
    tokens,
    cotangent,
    slot_tokens,
    slot_counts,
    slot_gates,
    swap_pairs,
    gate_weight,
    up_weight,
    down_weight,
    first_moment,
    second_moment,
):
    tok_count, model_cols = tokens.shape
    experts = slot_counts.shape[1]
    capacity = slot_tokens.shape[2]
    own_slots = capacity // 2
    rows = experts * own_slots
    pair_cols = 2 * model_cols
    chips = lax.axis_size("dp") // 2
    dp_pos = lax.axis_index("dp")
    core, y_pos = dp_pos % 2, dp_pos // 2
    position = lax.axis_index("expert")
    half_count = swap_pairs.shape[0]
    own_swap = (
        jnp.sum(jnp.where(jnp.arange(half_count) == position % half_count, swap_pairs, 0)) > 0
    )

    def own_part(table):
        return lax.dynamic_slice_in_dim(table, core * own_slots, own_slots, 1)

    live = (own_part(jnp.arange(capacity)[None, :]) < slot_counts[0][:, None]).reshape(-1)
    route = own_part(slot_tokens[0]).reshape(-1)
    weighted = jnp.where(live, own_part(slot_gates[0]).reshape(-1), 0.0)
    masked_route = jnp.where(live, route, -1)
    token_ids = jnp.arange(tok_count)

    def exchange(block):
        return lax.all_to_all(
            block.reshape(experts, own_slots, pair_cols), "expert", 0, 0, tiled=True
        ).reshape(rows, pair_cols)

    token_cols = pair_rows(tokens.T)
    pick = (masked_route[:, None] == token_ids[None, :]).astype(BF)
    arrived = exchange(dot(pick, token_cols, 1, 1).astype(BF))
    grad_cols = pair_rows(cotangent.T)
    grad_rows = (dot(pick, grad_cols, 1, 1) * weighted[:, None]).astype(BF)
    far_gate = core_swap(gate_weight[0])
    far_up = core_swap(up_weight[0])
    gate_up = join_weights(gate_weight[0], up_weight[0], far_gate, far_up)
    down_cols = pair_rows(down_weight[0].T)
    arrived, gate_up, down_cols, grad_rows = lax.optimization_barrier(
        (arrived, gate_up, down_cols, grad_rows)
    )
    moment_one = first_moment[0].T
    moment_two = second_moment[0].T
    arrived_grad = exchange(grad_rows)
    far_one = expert_swap(tie(moment_one, arrived).astype(BF))
    far_two = expert_swap(tie(moment_two, arrived).astype(BF))

    hidden_units = down_weight.shape[1]
    half = rows // (2 * chips)
    products = ordered_dot(y_pos, arrived, gate_up, RING_UNITS, (2 * half, 2 * half, 4 * half))
    preact = ring_sum(*products, chips)
    gate_pre, up_pre = preact[:, :hidden_units], preact[:, hidden_units:]
    sig = jax.nn.sigmoid(gate_pre)
    hidden_shard = (gate_pre * sig * up_pre).astype(BF)
    arrived_grad = tie(arrived_grad, hidden_shard)
    terms = ordered_dot(
        y_pos, arrived_grad, down_cols, ((2, 0), (1, 0), (3, 0), (0, 0)), (2 * half,) * 4
    )
    gathered = ring_gather(hidden_shard, chips)
    gathered = tie_all(gathered, *terms)
    out_rows, hidden = gathered_dot(y_pos, gathered, down_cols, True)
    returned = exchange(out_rows)

    hidden_grad = terms[3].astype(F32)
    for step, term in zip((2, 1, 3), terms):
        came = chip_shift(term, step)
        hidden_grad = hidden_grad + came.astype(F32)
    gate_grad = hidden_grad * up_pre * sig * (1.0 + gate_pre * (1.0 - sig))
    up_grad = hidden_grad * gate_pre * sig
    pre_shard = jnp.concatenate([gate_grad, up_grad], axis=1).astype(BF)
    weight_grad = pair_sum(dot(tie(arrived_grad, pre_shard), hidden, 0, 0))
    sent_grad = weight_grad.astype(BF)
    gathered = ring_gather(pre_shard, chips)
    gathered = tie_all(gathered, sent_grad)
    far_grad = expert_swap(sent_grad)
    (back,) = gathered_dot(y_pos, gathered, gate_up, False)
    returned_grad = exchange(back)

    one = jnp.where(own_swap, far_one.astype(F32), moment_one)
    two = jnp.where(own_swap, far_two.astype(F32), moment_two)
    grad = jnp.where(own_swap, far_grad.astype(F32), weight_grad)
    new_one = beta_first * one + (1.0 - beta_first) * grad
    new_two = beta_second * two + (1.0 - beta_second) * grad * grad
    step_dir = (new_one / (jnp.sqrt(new_two) + adam_eps)).astype(BF)

    match = masked_route[:, None] == token_ids[None, :]
    top = lax.reduce_precision(weighted, 8, 7)
    rest = weighted - top
    mixed = pair_sum(
        dot(returned, jnp.where(match, top[:, None], 0.0).astype(BF), 0, 0)
        + dot(returned, jnp.where(match, rest[:, None], 0.0).astype(BF), 0, 0),
    ).astype(BF)
    returned_grad = tie(returned_grad, mixed, step_dir)
    token_grad = pair_sum(dot(returned_grad, match.astype(BF), 0, 0)).astype(BF)
    return (mixed.T, token_grad.T, new_one.T[None], new_two.T[None], step_dir.T[None])


def solution(mesh):
    return jax.shard_map(
        shards,
        mesh=mesh,
        in_specs=(
            P("expert", "dp"),
            P("expert", "dp"),
            P("expert", None, None),
            P("expert", None),
            P("expert", None, None),
            P(),
            P("expert", "dp", None),
            P("expert", "dp", None),
            P("expert", None, "dp"),
            P("expert", None, "dp"),
            P("expert", None, "dp"),
        ),
        out_specs=(
            P("expert", "dp"),
            P("expert", "dp"),
            P("expert", None, "dp"),
            P("expert", None, "dp"),
            P("expert", None, "dp"),
        ),
        check_vma=False,
    )
```

```python
import jax
import jax.numpy as jnp
from jax import lax
from jax.experimental import pallas as pl
from jax.experimental.pallas import tpu as pltpu
from jax.sharding import PartitionSpec as P


beta_first = 0.9
beta_second = 0.999
adam_eps = 1e-08
BF = jnp.bfloat16
F32 = jnp.float32


def dot(a, b, ca=1, cb=0):
    return lax.dot_general(a, b, (((ca,), (cb,)), ((), ())), preferred_element_type=F32)


def core_swap(block):
    return lax.ppermute(block, "dp", [(i, i ^ 1) for i in range(lax.axis_size("dp"))])


def chip_shift(block, step):
    count = lax.axis_size("dp")
    return lax.ppermute(block, "dp", [(i, (i + 2 * step) % count) for i in range(count)])


def expert_swap(block):
    count = lax.axis_size("expert")
    return lax.ppermute(block, "expert", [(i, i ^ (count // 2)) for i in range(count)])


def tie(value, *others):
    return lax.optimization_barrier((value,) + others)[0]


def tie_all(values, *others):
    return lax.optimization_barrier(tuple(values) + others)[: len(values)]


def ordered_dot(y_pos, left, right, units, sizes):
    rows, depth = left.shape
    width = right.shape[1]
    unit = rows // len(units)
    per_block = len(units) // 4
    tile = 512

    def body(pos, left_ref, right_ref, *refs):
        outs, ordered = refs[:-1], refs[-1]

        @pl.when(pl.program_id(0) == 0)
        def _():
            for place, (step, part) in enumerate(units):
                at = (lax.rem(pos[0] + step, 4) * per_block + part) * unit
                ordered[place * unit : (place + 1) * unit, :] = left_ref[
                    pl.ds(pl.multiple_of(at, unit), unit), :
                ]

        start = 0
        for out in outs:
            size = out.shape[0]
            out[...] = dot(ordered[start : start + size, :], right_ref[...]).astype(BF)
            start += size

    return pl.pallas_call(
        body,
        out_shape=[pltpu.HBM((size, width), BF) for size in sizes],
        grid_spec=pltpu.PrefetchScalarGridSpec(
            num_scalar_prefetch=1,
            grid=(width // tile,),
            in_specs=[
                pl.BlockSpec((rows, depth), lambda i, pos: (0, 0)),
                pl.BlockSpec((depth, tile), lambda i, pos: (0, i)),
            ],
            out_specs=[pl.BlockSpec((size, tile), lambda i, pos: (0, i)) for size in sizes],
            scratch_shapes=[pltpu.VMEM((rows, depth), BF)],
        ),
        compiler_params=pltpu.CompilerParams(vmem_limit_bytes=16 << 20),
        cost_estimate=pl.CostEstimate(
            flops=2 * rows * depth * width,
            bytes_accessed=2 * (rows * depth + depth * width + rows * width),
            transcendentals=0,
        ),
    )(y_pos.reshape(1), left, pltpu.with_memory_space_constraint(right, pltpu.HBM))


def gathered_dot(y_pos, parts, right, keep):
    own, _, _, _, _ = parts
    rows, depth = own.shape
    width = right.shape[0]
    total = 4 * rows
    mid = rows // 2

    def body(pos, own_ref, left_ref, right_ref, top_ref, low_ref, w_ref, out, full):
        for step, offset, ref in (
            (0, 0, own_ref),
            (3, 0, left_ref),
            (1, 0, right_ref),
            (2, 0, top_ref),
            (2, mid, low_ref),
        ):
            at = lax.rem(pos[0] + step, 4) * rows + offset
            full[pl.ds(pl.multiple_of(at, mid), ref.shape[0]), :] = ref[...]
        out[...] = dot(full[...], w_ref[...], 1, 1).astype(BF)

    vmem = pl.BlockSpec(memory_space=pltpu.VMEM)
    out_shape = [pltpu.HBM((total, width), BF)]
    out_specs = [pl.BlockSpec((total, width), lambda k: (0, 0))]
    scratch = []
    if keep:
        out_shape.append(pltpu.HBM((total, depth), BF))
        out_specs.append(pl.BlockSpec((total, depth), lambda k: (0, 0)))
    else:
        scratch.append(pltpu.VMEM((total, depth), BF))
    return pl.pallas_call(
        body,
        out_shape=out_shape,
        grid=(1,),
        in_specs=[pl.BlockSpec(memory_space=pltpu.SMEM)] + [vmem] * 6,
        out_specs=out_specs,
        scratch_shapes=scratch,
        compiler_params=pltpu.CompilerParams(vmem_limit_bytes=24 << 20),
        cost_estimate=pl.CostEstimate(
            flops=2 * total * depth * width,
            bytes_accessed=2 * (total * depth + depth * width + total * width),
            transcendentals=0,
        ),
    )(y_pos.reshape(1), *parts, right)


RING_UNITS = ((2, 0), (1, 1), (2, 1), (3, 0), (0, 0), (0, 1), (1, 0), (3, 1))


def ring_sum(to_right, to_left, rest, chips):
    rows = rest.shape[0] // 4
    own_top, own_low, pass_right, pass_left = (rest[i * rows :][:rows] for i in range(4))
    from_left = chip_shift(to_right, 1)
    from_right = chip_shift(to_left, chips - 1)
    on_right = (pass_right.astype(F32) + from_left[:rows].astype(F32)).astype(BF)
    on_left = (pass_left.astype(F32) + from_right[:rows].astype(F32)).astype(BF)
    on_right, on_left = lax.optimization_barrier((on_right, on_left))
    far_left = chip_shift(on_right, 1)
    far_right = chip_shift(on_left, chips - 1)
    top = own_top.astype(F32) + from_right[rows:].astype(F32) + far_left.astype(F32)
    low = own_low.astype(F32) + from_left[rows:].astype(F32) + far_right.astype(F32)
    return jnp.concatenate([top, low])


def ring_gather(shard, chips):
    mid = shard.shape[0] // 2
    left = chip_shift(shard, 1)
    right = chip_shift(shard, chips - 1)
    far_top = chip_shift(left[:mid], 1)
    far_low = chip_shift(right[mid:], chips - 1)
    return shard, left, right, far_top, far_low


def pair_rows(block):
    far = core_swap(block)
    return jnp.concatenate([block, far], axis=0)


def join_weights(gate_own, up_own, gate_far, up_far):
    rows, units = gate_own.shape
    steps = 4
    block = rows // steps

    def body(gate_a, up_a, gate_b, up_b, out):
        first = pl.program_id(0) < steps

        @pl.when(first)
        def _():
            out[:, :units] = gate_a[...]
            out[:, units:] = up_a[...]

        @pl.when(jnp.logical_not(first))
        def _():
            out[:, :units] = gate_b[...]
            out[:, units:] = up_b[...]

    near = pl.BlockSpec((block, units), lambda i: (jnp.minimum(i, steps - 1), 0))
    far = pl.BlockSpec((block, units), lambda i: (jnp.maximum(i - steps, 0), 0))
    moved = 8 * rows * units
    return pl.pallas_call(
        body,
        out_shape=pltpu.HBM((2 * rows, 2 * units), gate_own.dtype),
        grid=(2 * steps,),
        in_specs=[near, near, far, far],
        out_specs=pl.BlockSpec((block, 2 * units), lambda i: (i, 0)),
        compiler_params=pltpu.CompilerParams(vmem_limit_bytes=8 << 20),
        cost_estimate=pl.CostEstimate(flops=0, bytes_accessed=2 * moved, transcendentals=0),
    )(gate_own, up_own, gate_far, up_far)


def pair_sum(partial):
    split = partial.shape[0] // 2
    far = core_swap(partial[split:].astype(BF))
    return partial[:split] + far.astype(F32)


def shards(
    tokens,
    cotangent,
    slot_tokens,
    slot_counts,
    slot_gates,
    swap_pairs,
    gate_weight,
    up_weight,
    down_weight,
    first_moment,
    second_moment,
):
    tok_count, model_cols = tokens.shape
    experts = slot_counts.shape[1]
    capacity = slot_tokens.shape[2]
    own_slots = capacity // 2
    rows = experts * own_slots
    pair_cols = 2 * model_cols
    chips = lax.axis_size("dp") // 2
    dp_pos = lax.axis_index("dp")
    core, y_pos = dp_pos % 2, dp_pos // 2
    position = lax.axis_index("expert")
    half_count = swap_pairs.shape[0]
    own_swap = (
        jnp.sum(jnp.where(jnp.arange(half_count) == position % half_count, swap_pairs, 0)) > 0
    )

    def own_part(table):
        return lax.dynamic_slice_in_dim(table, core * own_slots, own_slots, 1)

    live = (own_part(jnp.arange(capacity)[None, :]) < slot_counts[0][:, None]).reshape(-1)
    route = own_part(slot_tokens[0]).reshape(-1)
    weighted = jnp.where(live, own_part(slot_gates[0]).reshape(-1), 0.0)
    masked_route = jnp.where(live, route, -1)
    token_ids = jnp.arange(tok_count)

    def exchange(block):
        return lax.all_to_all(
            block.reshape(experts, own_slots, pair_cols), "expert", 0, 0, tiled=True
        ).reshape(rows, pair_cols)

    token_cols = pair_rows(tokens.T)
    pick = (masked_route[:, None] == token_ids[None, :]).astype(BF)
    arrived = exchange(dot(pick, token_cols, 1, 1).astype(BF))
    grad_cols = pair_rows(cotangent.T)
    grad_rows = (dot(pick, grad_cols, 1, 1) * weighted[:, None]).astype(BF)
    far_gate = core_swap(gate_weight[0])
    far_up = core_swap(up_weight[0])
    gate_up = join_weights(gate_weight[0], up_weight[0], far_gate, far_up)
    down_cols = pair_rows(down_weight[0].T)
    moment_one = first_moment[0].T
    moment_two = second_moment[0].T
    far_one = expert_swap(tie(moment_one, grad_cols).astype(BF))
    far_two = expert_swap(tie(moment_two, grad_cols).astype(BF))

    arrived, gate_up, down_cols, grad_rows = lax.optimization_barrier(
        (arrived, gate_up, down_cols, grad_rows)
    )
    arrived_grad = exchange(grad_rows)
    hidden_units = down_weight.shape[1]
    half = rows // (2 * chips)
    products = ordered_dot(y_pos, arrived, gate_up, RING_UNITS, (2 * half, 2 * half, 4 * half))
    preact = ring_sum(*products, chips)
    gate_pre, up_pre = preact[:, :hidden_units], preact[:, hidden_units:]
    sig = jax.nn.sigmoid(gate_pre)
    hidden_shard = (gate_pre * sig * up_pre).astype(BF)
    arrived_grad = tie(arrived_grad, hidden_shard)
    terms = ordered_dot(
        y_pos, arrived_grad, down_cols, ((2, 0), (1, 0), (3, 0), (0, 0)), (2 * half,) * 4
    )
    gathered = ring_gather(hidden_shard, chips)
    gathered = tie_all(gathered, *terms)
    out_rows, hidden = gathered_dot(y_pos, gathered, down_cols, True)
    returned = exchange(out_rows)

    hidden_grad = terms[3].astype(F32)
    for step, term in zip((2, 1, 3), terms):
        came = chip_shift(term, step)
        hidden_grad = hidden_grad + came.astype(F32)
    gate_grad = hidden_grad * up_pre * sig * (1.0 + gate_pre * (1.0 - sig))
    up_grad = hidden_grad * gate_pre * sig
    pre_shard = jnp.concatenate([gate_grad, up_grad], axis=1).astype(BF)
    weight_grad = pair_sum(dot(tie(arrived_grad, pre_shard), hidden, 0, 0))
    sent_grad = weight_grad.astype(BF)
    gathered = ring_gather(pre_shard, chips)
    gathered = tie_all(gathered, sent_grad)
    far_grad = expert_swap(sent_grad)
    (back,) = gathered_dot(y_pos, gathered, gate_up, False)
    returned_grad = exchange(back)

    one = jnp.where(own_swap, far_one.astype(F32), moment_one)
    two = jnp.where(own_swap, far_two.astype(F32), moment_two)
    grad = jnp.where(own_swap, far_grad.astype(F32), weight_grad)
    new_one = beta_first * one + (1.0 - beta_first) * grad
    new_two = beta_second * two + (1.0 - beta_second) * grad * grad
    step_dir = (new_one / (jnp.sqrt(new_two) + adam_eps)).astype(BF)

    match = masked_route[:, None] == token_ids[None, :]
    top = lax.reduce_precision(weighted, 8, 7)
    rest = weighted - top
    mixed = pair_sum(
        dot(returned, jnp.where(match, top[:, None], 0.0).astype(BF), 0, 0)
        + dot(returned, jnp.where(match, rest[:, None], 0.0).astype(BF), 0, 0),
    ).astype(BF)
    returned_grad = tie(returned_grad, mixed, step_dir)
    token_grad = pair_sum(dot(returned_grad, match.astype(BF), 0, 0)).astype(BF)
    return (mixed.T, token_grad.T, new_one.T[None], new_two.T[None], step_dir.T[None])


def solution(mesh):
    return jax.shard_map(
        shards,
        mesh=mesh,
        in_specs=(
            P("expert", "dp"),
            P("expert", "dp"),
            P("expert", None, None),
            P("expert", None),
            P("expert", None, None),
            P(),
            P("expert", "dp", None),
            P("expert", "dp", None),
            P("expert", None, "dp"),
            P("expert", None, "dp"),
            P("expert", None, "dp"),
        ),
        out_specs=(
            P("expert", "dp"),
            P("expert", "dp"),
            P("expert", None, "dp"),
            P("expert", None, "dp"),
            P("expert", None, "dp"),
        ),
        check_vma=False,
    )
```

```python
import jax
import jax.numpy as jnp
from jax import lax
from jax.experimental import pallas as pl
from jax.experimental.pallas import tpu as pltpu
from jax.sharding import PartitionSpec as P


beta_first = 0.9
beta_second = 0.999
adam_eps = 1e-08
BF = jnp.bfloat16
F32 = jnp.float32


def dot(a, b, ca=1, cb=0):
    return lax.dot_general(a, b, (((ca,), (cb,)), ((), ())), preferred_element_type=F32)


def core_swap(block):
    return lax.ppermute(block, "dp", [(i, i ^ 1) for i in range(lax.axis_size("dp"))])


def chip_shift(block, step):
    count = lax.axis_size("dp")
    return lax.ppermute(block, "dp", [(i, (i + 2 * step) % count) for i in range(count)])


def expert_swap(block):
    count = lax.axis_size("expert")
    return lax.ppermute(block, "expert", [(i, i ^ (count // 2)) for i in range(count)])


def tie(value, *others):
    return lax.optimization_barrier((value,) + others)[0]


def tie_all(values, *others):
    return lax.optimization_barrier(tuple(values) + others)[: len(values)]


def ordered_dot(y_pos, left, right, units, sizes):
    rows, depth = left.shape
    width = right.shape[1]
    unit = rows // len(units)
    per_block = len(units) // 4
    tile = 512

    def body(pos, left_ref, right_ref, *refs):
        outs, ordered = refs[:-1], refs[-1]

        @pl.when(pl.program_id(0) == 0)
        def _():
            for place, (step, part) in enumerate(units):
                at = (lax.rem(pos[0] + step, 4) * per_block + part) * unit
                ordered[place * unit : (place + 1) * unit, :] = left_ref[
                    pl.ds(pl.multiple_of(at, unit), unit), :
                ]

        product = dot(ordered[...], right_ref[...]).astype(BF)
        start = 0
        for out in outs:
            out[...] = product[start : start + out.shape[0], :]
            start += out.shape[0]

    return pl.pallas_call(
        body,
        out_shape=[pltpu.HBM((size, width), BF) for size in sizes],
        grid_spec=pltpu.PrefetchScalarGridSpec(
            num_scalar_prefetch=1,
            grid=(width // tile,),
            in_specs=[
                pl.BlockSpec((rows, depth), lambda i, pos: (0, 0)),
                pl.BlockSpec((depth, tile), lambda i, pos: (0, i)),
            ],
            out_specs=[pl.BlockSpec((size, tile), lambda i, pos: (0, i)) for size in sizes],
            scratch_shapes=[pltpu.VMEM((rows, depth), BF)],
        ),
        compiler_params=pltpu.CompilerParams(vmem_limit_bytes=16 << 20),
        cost_estimate=pl.CostEstimate(
            flops=2 * rows * depth * width,
            bytes_accessed=2 * (rows * depth + depth * width + rows * width),
            transcendentals=0,
        ),
    )(y_pos.reshape(1), left, pltpu.with_memory_space_constraint(right, pltpu.HBM))


def gathered_dot(y_pos, parts, right, keep):
    rows, depth = parts[0].shape
    width = right.shape[0]
    total = 4 * rows
    mid = rows // 2

    def body(pos, *refs):
        w_ref, out, full = refs[len(parts) :]
        for (step, offset), ref in zip(((0, 0), (3, 0), (1, 0), (2, 0), (2, mid)), refs[: len(parts)]):
            at = lax.rem(pos[0] + step, 4) * rows + offset
            full[pl.ds(pl.multiple_of(at, mid), ref.shape[0]), :] = ref[...]
        out[...] = dot(full[...], w_ref[...], 1, 1).astype(BF)

    vmem = pl.BlockSpec(memory_space=pltpu.VMEM)
    out_shape = [pltpu.HBM((total, width), BF)]
    out_specs = [pl.BlockSpec((total, width), lambda k: (0, 0))]
    scratch = []
    if keep:
        out_shape.append(pltpu.HBM((total, depth), BF))
        out_specs.append(pl.BlockSpec((total, depth), lambda k: (0, 0)))
    else:
        scratch.append(pltpu.VMEM((total, depth), BF))
    return pl.pallas_call(
        body,
        out_shape=out_shape,
        grid=(1,),
        in_specs=[pl.BlockSpec(memory_space=pltpu.SMEM)] + [vmem] * (len(parts) + 1),
        out_specs=out_specs,
        scratch_shapes=scratch,
        compiler_params=pltpu.CompilerParams(vmem_limit_bytes=24 << 20),
        cost_estimate=pl.CostEstimate(
            flops=2 * total * depth * width,
            bytes_accessed=2 * (total * depth + depth * width + total * width),
            transcendentals=0,
        ),
    )(y_pos.reshape(1), *parts, right)


RING_UNITS = ((2, 0), (1, 1), (2, 1), (3, 0), (0, 0), (0, 1), (1, 0), (3, 1))


def ring_sum(to_right, to_left, rest, chips):
    rows = rest.shape[0] // 4
    own_top, own_low, pass_right, pass_left = (rest[i * rows :][:rows] for i in range(4))
    from_left = chip_shift(to_right, 1)
    from_right = chip_shift(to_left, chips - 1)
    on_right = (pass_right.astype(F32) + from_left[:rows].astype(F32)).astype(BF)
    on_left = (pass_left.astype(F32) + from_right[:rows].astype(F32)).astype(BF)
    on_right, on_left = lax.optimization_barrier((on_right, on_left))
    far_left = chip_shift(on_right, 1)
    far_right = chip_shift(on_left, chips - 1)
    top = own_top.astype(F32) + from_right[rows:].astype(F32) + far_left.astype(F32)
    low = own_low.astype(F32) + from_left[rows:].astype(F32) + far_right.astype(F32)
    return jnp.concatenate([top, low])


def direct_gather(shard):
    came = {}
    for step in (2, 1, 3):
        came[step] = chip_shift(shard, step)
    return shard, came[1], came[3], came[2]


def ring_gather(shard, chips):
    mid = shard.shape[0] // 2
    left = chip_shift(shard, 1)
    right = chip_shift(shard, chips - 1)
    far_top = chip_shift(left[:mid], 1)
    far_low = chip_shift(right[mid:], chips - 1)
    return shard, left, right, far_top, far_low


def pair_rows(block):
    far = core_swap(block)
    return jnp.concatenate([block, far], axis=0)


def join_weights(gate_own, up_own, gate_far, up_far):
    rows, units = gate_own.shape
    steps = 4
    block = rows // steps

    def body(gate_a, up_a, gate_b, up_b, out):
        first = pl.program_id(0) < steps

        @pl.when(first)
        def _():
            out[:, :units] = gate_a[...]
            out[:, units:] = up_a[...]

        @pl.when(jnp.logical_not(first))
        def _():
            out[:, :units] = gate_b[...]
            out[:, units:] = up_b[...]

    near = pl.BlockSpec((block, units), lambda i: (jnp.minimum(i, steps - 1), 0))
    far = pl.BlockSpec((block, units), lambda i: (jnp.maximum(i - steps, 0), 0))
    moved = 8 * rows * units
    return pl.pallas_call(
        body,
        out_shape=pltpu.HBM((2 * rows, 2 * units), gate_own.dtype),
        grid=(2 * steps,),
        in_specs=[near, near, far, far],
        out_specs=pl.BlockSpec((block, 2 * units), lambda i: (i, 0)),
        compiler_params=pltpu.CompilerParams(vmem_limit_bytes=8 << 20),
        cost_estimate=pl.CostEstimate(flops=0, bytes_accessed=2 * moved, transcendentals=0),
    )(gate_own, up_own, gate_far, up_far)


def pair_sum(partial):
    split = partial.shape[0] // 2
    far = core_swap(partial[split:].astype(BF))
    return partial[:split] + far.astype(F32)


def shards(
    tokens,
    cotangent,
    slot_tokens,
    slot_counts,
    slot_gates,
    swap_pairs,
    gate_weight,
    up_weight,
    down_weight,
    first_moment,
    second_moment,
):
    tok_count, model_cols = tokens.shape
    experts = slot_counts.shape[1]
    capacity = slot_tokens.shape[2]
    own_slots = capacity // 2
    rows = experts * own_slots
    pair_cols = 2 * model_cols
    chips = lax.axis_size("dp") // 2
    dp_pos = lax.axis_index("dp")
    core, y_pos = dp_pos % 2, dp_pos // 2
    position = lax.axis_index("expert")
    half_count = swap_pairs.shape[0]
    own_swap = (
        jnp.sum(jnp.where(jnp.arange(half_count) == position % half_count, swap_pairs, 0)) > 0
    )

    def own_part(table):
        return lax.dynamic_slice_in_dim(table, core * own_slots, own_slots, 1)

    live = (own_part(jnp.arange(capacity)[None, :]) < slot_counts[0][:, None]).reshape(-1)
    route = own_part(slot_tokens[0]).reshape(-1)
    weighted = jnp.where(live, own_part(slot_gates[0]).reshape(-1), 0.0)
    masked_route = jnp.where(live, route, -1)
    token_ids = jnp.arange(tok_count)

    def exchange(block):
        return lax.all_to_all(
            block.reshape(experts, own_slots, pair_cols), "expert", 0, 0, tiled=True
        ).reshape(rows, pair_cols)

    token_cols = pair_rows(tokens.T)
    pick = (masked_route[:, None] == token_ids[None, :]).astype(BF)
    arrived = exchange(dot(pick, token_cols, 1, 1).astype(BF))
    grad_cols = pair_rows(cotangent.T)
    grad_rows = (dot(pick, grad_cols, 1, 1) * weighted[:, None]).astype(BF)
    far_gate = core_swap(gate_weight[0])
    far_up = core_swap(up_weight[0])
    gate_up = join_weights(gate_weight[0], up_weight[0], far_gate, far_up)
    down_cols = pair_rows(down_weight[0].T)
    moment_one = first_moment[0].T
    moment_two = second_moment[0].T
    far_one = expert_swap(tie(moment_one, grad_cols).astype(BF))
    far_two = expert_swap(tie(moment_two, grad_cols).astype(BF))

    arrived, gate_up, down_cols, grad_rows = lax.optimization_barrier(
        (arrived, gate_up, down_cols, grad_rows)
    )
    arrived_grad = exchange(grad_rows)
    hidden_units = down_weight.shape[1]
    half = rows // (2 * chips)
    products = ordered_dot(y_pos, arrived, gate_up, RING_UNITS, (2 * half, 2 * half, 4 * half))
    preact = ring_sum(*products, chips)
    gate_pre, up_pre = preact[:, :hidden_units], preact[:, hidden_units:]
    sig = jax.nn.sigmoid(gate_pre)
    hidden_shard = (gate_pre * sig * up_pre).astype(BF)
    arrived_grad = tie(arrived_grad, hidden_shard)
    terms = ordered_dot(
        y_pos, arrived_grad, down_cols, ((2, 0), (1, 0), (3, 0), (0, 0)), (2 * half,) * 4
    )
    gathered = direct_gather(hidden_shard)
    gathered = tie_all(gathered, *terms)
    out_rows, hidden = gathered_dot(y_pos, gathered, down_cols, True)
    returned = exchange(out_rows)

    hidden_grad = terms[3].astype(F32)
    for step, term in zip((2, 1, 3), terms):
        came = chip_shift(term, step)
        hidden_grad = hidden_grad + came.astype(F32)
    gate_grad = hidden_grad * up_pre * sig * (1.0 + gate_pre * (1.0 - sig))
    up_grad = hidden_grad * gate_pre * sig
    pre_shard = jnp.concatenate([gate_grad, up_grad], axis=1).astype(BF)
    weight_grad = pair_sum(dot(tie(arrived_grad, pre_shard), hidden, 0, 0))
    sent_grad = weight_grad.astype(BF)
    gathered = ring_gather(pre_shard, chips)
    gathered = tie_all(gathered, sent_grad)
    far_grad = expert_swap(sent_grad)
    (back,) = gathered_dot(y_pos, gathered, gate_up, False)
    returned_grad = exchange(back)

    one = jnp.where(own_swap, far_one.astype(F32), moment_one)
    two = jnp.where(own_swap, far_two.astype(F32), moment_two)
    grad = jnp.where(own_swap, far_grad.astype(F32), weight_grad)
    new_one = beta_first * one + (1.0 - beta_first) * grad
    new_two = beta_second * two + (1.0 - beta_second) * grad * grad
    step_dir = (new_one / (jnp.sqrt(new_two) + adam_eps)).astype(BF)

    match = masked_route[:, None] == token_ids[None, :]
    top = lax.reduce_precision(weighted, 8, 7)
    rest = weighted - top
    mixed = pair_sum(
        dot(returned, jnp.where(match, top[:, None], 0.0).astype(BF), 0, 0)
        + dot(returned, jnp.where(match, rest[:, None], 0.0).astype(BF), 0, 0),
    ).astype(BF)
    returned_grad = tie(returned_grad, mixed, step_dir)
    token_grad = pair_sum(dot(returned_grad, match.astype(BF), 0, 0)).astype(BF)
    return (mixed.T, token_grad.T, new_one.T[None], new_two.T[None], step_dir.T[None])


def solution(mesh):
    return jax.shard_map(
        shards,
        mesh=mesh,
        in_specs=(
            P("expert", "dp"),
            P("expert", "dp"),
            P("expert", None, None),
            P("expert", None),
            P("expert", None, None),
            P(),
            P("expert", "dp", None),
            P("expert", "dp", None),
            P("expert", None, "dp"),
            P("expert", None, "dp"),
            P("expert", None, "dp"),
        ),
        out_specs=(
            P("expert", "dp"),
            P("expert", "dp"),
            P("expert", None, "dp"),
            P("expert", None, "dp"),
            P("expert", None, "dp"),
        ),
        check_vma=False,
    )
```

```python
import jax
import jax.numpy as jnp
from jax import lax
from jax.experimental import pallas as pl
from jax.experimental.pallas import tpu as pltpu
from jax.sharding import PartitionSpec as P


beta_first = 0.9
beta_second = 0.999
adam_eps = 1e-08
BF = jnp.bfloat16
F32 = jnp.float32


def dot(a, b, ca=1, cb=0):
    return lax.dot_general(a, b, (((ca,), (cb,)), ((), ())), preferred_element_type=F32)


def core_swap(block):
    return lax.ppermute(block, "dp", [(i, i ^ 1) for i in range(lax.axis_size("dp"))])


def chip_shift(block, step):
    count = lax.axis_size("dp")
    return lax.ppermute(block, "dp", [(i, (i + 2 * step) % count) for i in range(count)])


def expert_swap(block):
    count = lax.axis_size("expert")
    return lax.ppermute(block, "expert", [(i, i ^ (count // 2)) for i in range(count)])


def tie(value, *others):
    return lax.optimization_barrier((value,) + others)[0]


def tie_all(values, *others):
    return lax.optimization_barrier(tuple(values) + others)[: len(values)]


def ordered_dot(y_pos, left, right, units, sizes):
    rows, depth = left.shape
    width = right.shape[1]
    unit = rows // len(units)
    per_block = len(units) // 4
    tile = 512

    def body(pos, left_ref, right_ref, *refs):
        outs, ordered = refs[:-1], refs[-1]

        @pl.when(pl.program_id(0) == 0)
        def _():
            for place, (step, part) in enumerate(units):
                at = (lax.rem(pos[0] + step, 4) * per_block + part) * unit
                ordered[place * unit : (place + 1) * unit, :] = left_ref[
                    pl.ds(pl.multiple_of(at, unit), unit), :
                ]

        product = dot(ordered[...], right_ref[...]).astype(BF)
        start = 0
        for out in outs:
            out[...] = product[start : start + out.shape[0], :]
            start += out.shape[0]

    return pl.pallas_call(
        body,
        out_shape=[pltpu.HBM((size, width), BF) for size in sizes],
        grid_spec=pltpu.PrefetchScalarGridSpec(
            num_scalar_prefetch=1,
            grid=(width // tile,),
            in_specs=[
                pl.BlockSpec((rows, depth), lambda i, pos: (0, 0)),
                pl.BlockSpec((depth, tile), lambda i, pos: (0, i)),
            ],
            out_specs=[pl.BlockSpec((size, tile), lambda i, pos: (0, i)) for size in sizes],
            scratch_shapes=[pltpu.VMEM((rows, depth), BF)],
        ),
        compiler_params=pltpu.CompilerParams(vmem_limit_bytes=16 << 20),
        cost_estimate=pl.CostEstimate(
            flops=2 * rows * depth * width,
            bytes_accessed=2 * (rows * depth + depth * width + rows * width),
            transcendentals=0,
        ),
    )(y_pos.reshape(1), left, pltpu.with_memory_space_constraint(right, pltpu.HBM))


def gathered_dot(y_pos, parts, right, keep):
    rows, depth = parts[0].shape
    width = right.shape[0]
    total = 4 * rows
    mid = rows // 2

    def body(pos, *refs):
        w_ref, out, full = refs[len(parts) :]
        for (step, offset), ref in zip(((0, 0), (3, 0), (1, 0), (2, 0), (2, mid)), refs[: len(parts)]):
            at = lax.rem(pos[0] + step, 4) * rows + offset
            full[pl.ds(pl.multiple_of(at, mid), ref.shape[0]), :] = ref[...]
        out[...] = dot(full[...], w_ref[...], 1, 1).astype(BF)

    vmem = pl.BlockSpec(memory_space=pltpu.VMEM)
    out_shape = [pltpu.HBM((total, width), BF)]
    out_specs = [pl.BlockSpec((total, width), lambda k: (0, 0))]
    scratch = []
    if keep:
        out_shape.append(pltpu.HBM((total, depth), BF))
        out_specs.append(pl.BlockSpec((total, depth), lambda k: (0, 0)))
    else:
        scratch.append(pltpu.VMEM((total, depth), BF))
    return pl.pallas_call(
        body,
        out_shape=out_shape,
        grid=(1,),
        in_specs=[pl.BlockSpec(memory_space=pltpu.SMEM)] + [vmem] * (len(parts) + 1),
        out_specs=out_specs,
        scratch_shapes=scratch,
        compiler_params=pltpu.CompilerParams(vmem_limit_bytes=24 << 20),
        cost_estimate=pl.CostEstimate(
            flops=2 * total * depth * width,
            bytes_accessed=2 * (total * depth + depth * width + total * width),
            transcendentals=0,
        ),
    )(y_pos.reshape(1), *parts, right)


RING_UNITS = ((2, 0), (1, 1), (2, 1), (3, 0), (0, 0), (0, 1), (1, 0), (3, 1))


def ring_sum(to_right, to_left, rest, chips):
    rows = rest.shape[0] // 4
    own_top, own_low, pass_right, pass_left = (rest[i * rows :][:rows] for i in range(4))
    from_left = chip_shift(to_right, 1)
    from_right = chip_shift(to_left, chips - 1)
    on_right = (pass_right.astype(F32) + from_left[:rows].astype(F32)).astype(BF)
    on_left = (pass_left.astype(F32) + from_right[:rows].astype(F32)).astype(BF)
    on_right, on_left = lax.optimization_barrier((on_right, on_left))
    far_left = chip_shift(on_right, 1)
    far_right = chip_shift(on_left, chips - 1)
    top = own_top.astype(F32) + from_right[rows:].astype(F32) + far_left.astype(F32)
    low = own_low.astype(F32) + from_left[rows:].astype(F32) + far_right.astype(F32)
    return jnp.concatenate([top, low])


def direct_gather(shard):
    came = {}
    for step in (2, 1, 3):
        came[step] = chip_shift(shard, step)
    return shard, came[1], came[3], came[2]


def ring_gather(shard, chips):
    mid = shard.shape[0] // 2
    left = chip_shift(shard, 1)
    right = chip_shift(shard, chips - 1)
    far_top = chip_shift(left[:mid], 1)
    far_low = chip_shift(right[mid:], chips - 1)
    return shard, left, right, far_top, far_low


def pair_rows(block):
    far = core_swap(block)
    return jnp.concatenate([block, far], axis=0)


def join_weights(gate_own, up_own, gate_far, up_far):
    rows, units = gate_own.shape
    steps = 4
    block = rows // steps

    def body(gate_a, up_a, gate_b, up_b, out):
        first = pl.program_id(0) < steps

        @pl.when(first)
        def _():
            out[:, :units] = gate_a[...]
            out[:, units:] = up_a[...]

        @pl.when(jnp.logical_not(first))
        def _():
            out[:, :units] = gate_b[...]
            out[:, units:] = up_b[...]

    near = pl.BlockSpec((block, units), lambda i: (jnp.minimum(i, steps - 1), 0))
    far = pl.BlockSpec((block, units), lambda i: (jnp.maximum(i - steps, 0), 0))
    moved = 8 * rows * units
    return pl.pallas_call(
        body,
        out_shape=pltpu.HBM((2 * rows, 2 * units), gate_own.dtype),
        grid=(2 * steps,),
        in_specs=[near, near, far, far],
        out_specs=pl.BlockSpec((block, 2 * units), lambda i: (i, 0)),
        compiler_params=pltpu.CompilerParams(vmem_limit_bytes=8 << 20),
        cost_estimate=pl.CostEstimate(flops=0, bytes_accessed=2 * moved, transcendentals=0),
    )(gate_own, up_own, gate_far, up_far)


def pair_sum(partial):
    split = partial.shape[0] // 2
    far = core_swap(partial[split:].astype(BF))
    return partial[:split] + far.astype(F32)


def shards(
    tokens,
    cotangent,
    slot_tokens,
    slot_counts,
    slot_gates,
    swap_pairs,
    gate_weight,
    up_weight,
    down_weight,
    first_moment,
    second_moment,
):
    tok_count, model_cols = tokens.shape
    experts = slot_counts.shape[1]
    capacity = slot_tokens.shape[2]
    own_slots = capacity // 2
    rows = experts * own_slots
    pair_cols = 2 * model_cols
    chips = lax.axis_size("dp") // 2
    dp_pos = lax.axis_index("dp")
    core, y_pos = dp_pos % 2, dp_pos // 2
    position = lax.axis_index("expert")
    half_count = swap_pairs.shape[0]
    own_swap = (
        jnp.sum(jnp.where(jnp.arange(half_count) == position % half_count, swap_pairs, 0)) > 0
    )

    def own_part(table):
        return lax.dynamic_slice_in_dim(table, core * own_slots, own_slots, 1)

    live = (own_part(jnp.arange(capacity)[None, :]) < slot_counts[0][:, None]).reshape(-1)
    route = own_part(slot_tokens[0]).reshape(-1)
    weighted = jnp.where(live, own_part(slot_gates[0]).reshape(-1), 0.0)
    masked_route = jnp.where(live, route, -1)
    token_ids = jnp.arange(tok_count)

    def exchange(block):
        return lax.all_to_all(
            block.reshape(experts, own_slots, pair_cols), "expert", 0, 0, tiled=True
        ).reshape(rows, pair_cols)

    token_cols = pair_rows(tokens.T)
    pick = lax.optimization_barrier((masked_route[:, None] == token_ids[None, :]).astype(BF))
    arrived = exchange(dot(pick, token_cols, 1, 1).astype(BF))
    grad_cols = pair_rows(cotangent.T)
    grad_rows = (dot(pick, grad_cols, 1, 1) * weighted[:, None]).astype(BF)
    far_gate = core_swap(gate_weight[0])
    far_up = core_swap(up_weight[0])
    gate_up = join_weights(gate_weight[0], up_weight[0], far_gate, far_up)
    down_cols = pair_rows(down_weight[0].T)
    moment_one = first_moment[0].T
    moment_two = second_moment[0].T
    far_one = expert_swap(tie(moment_one, grad_cols).astype(BF))
    far_two = expert_swap(tie(moment_two, grad_cols).astype(BF))

    arrived, gate_up, down_cols, grad_rows = lax.optimization_barrier(
        (arrived, gate_up, down_cols, grad_rows)
    )
    arrived_grad = exchange(grad_rows)
    hidden_units = down_weight.shape[1]
    half = rows // (2 * chips)
    products = ordered_dot(y_pos, arrived, gate_up, RING_UNITS, (2 * half, 2 * half, 4 * half))
    preact = ring_sum(*products, chips)
    gate_pre, up_pre = preact[:, :hidden_units], preact[:, hidden_units:]
    sig = jax.nn.sigmoid(gate_pre)
    hidden_shard = (gate_pre * sig * up_pre).astype(BF)
    arrived_grad = tie(arrived_grad, hidden_shard)
    terms = ordered_dot(
        y_pos, arrived_grad, down_cols, ((2, 0), (1, 0), (3, 0), (0, 0)), (2 * half,) * 4
    )
    gathered = direct_gather(hidden_shard)
    gathered = tie_all(gathered, *terms)
    out_rows, hidden = gathered_dot(y_pos, gathered, down_cols, True)
    returned = exchange(out_rows)

    hidden_grad = terms[3].astype(F32)
    for step, term in zip((2, 1, 3), terms):
        came = chip_shift(term, step)
        hidden_grad = hidden_grad + came.astype(F32)
    gate_grad = hidden_grad * up_pre * sig * (1.0 + gate_pre * (1.0 - sig))
    up_grad = hidden_grad * gate_pre * sig
    pre_shard = jnp.concatenate([gate_grad, up_grad], axis=1).astype(BF)
    weight_grad = pair_sum(dot(tie(arrived_grad, pre_shard), hidden, 0, 0))
    sent_grad = weight_grad.astype(BF)
    gathered = ring_gather(pre_shard, chips)
    gathered = tie_all(gathered, sent_grad)
    far_grad = expert_swap(sent_grad)
    (back,) = gathered_dot(y_pos, gathered, gate_up, False)
    returned_grad = exchange(back)

    one = jnp.where(own_swap, far_one.astype(F32), moment_one)
    two = jnp.where(own_swap, far_two.astype(F32), moment_two)
    grad = jnp.where(own_swap, far_grad.astype(F32), weight_grad)
    new_one = beta_first * one + (1.0 - beta_first) * grad
    new_two = beta_second * two + (1.0 - beta_second) * grad * grad
    step_dir = (new_one / (jnp.sqrt(new_two) + adam_eps)).astype(BF)

    match = masked_route[:, None] == token_ids[None, :]
    top = lax.reduce_precision(weighted, 8, 7)
    rest = weighted - top
    mixed = pair_sum(
        dot(returned, jnp.where(match, top[:, None], 0.0).astype(BF), 0, 0)
        + dot(returned, jnp.where(match, rest[:, None], 0.0).astype(BF), 0, 0),
    ).astype(BF)
    hits = lax.optimization_barrier(match.astype(BF))
    returned_grad = tie(returned_grad, mixed, step_dir, hits)
    far_part = dot(returned_grad[:, model_cols:], hits, 0, 0).astype(BF)
    came = core_swap(far_part)
    near_part = lax.optimization_barrier(dot(returned_grad[:, :model_cols], hits, 0, 0))
    token_grad = (near_part + came.astype(F32)).astype(BF)
    return (mixed.T, token_grad.T, new_one.T[None], new_two.T[None], step_dir.T[None])


def solution(mesh):
    return jax.shard_map(
        shards,
        mesh=mesh,
        in_specs=(
            P("expert", "dp"),
            P("expert", "dp"),
            P("expert", None, None),
            P("expert", None),
            P("expert", None, None),
            P(),
            P("expert", "dp", None),
            P("expert", "dp", None),
            P("expert", None, "dp"),
            P("expert", None, "dp"),
            P("expert", None, "dp"),
        ),
        out_specs=(
            P("expert", "dp"),
            P("expert", "dp"),
            P("expert", None, "dp"),
            P("expert", None, "dp"),
            P("expert", None, "dp"),
        ),
        check_vma=False,
    )
```

```python
import jax
import jax.numpy as jnp
from jax import lax
from jax.experimental import pallas as pl
from jax.experimental.pallas import tpu as pltpu
from jax.sharding import PartitionSpec as P


beta_first = 0.9
beta_second = 0.999
adam_eps = 1e-08
BF = jnp.bfloat16
F32 = jnp.float32


def dot(a, b, ca=1, cb=0):
    return lax.dot_general(a, b, (((ca,), (cb,)), ((), ())), preferred_element_type=F32)


def core_swap(block):
    return lax.ppermute(block, "dp", [(i, i ^ 1) for i in range(lax.axis_size("dp"))])


def chip_shift(block, step):
    count = lax.axis_size("dp")
    return lax.ppermute(block, "dp", [(i, (i + 2 * step) % count) for i in range(count)])


def expert_swap(block):
    count = lax.axis_size("expert")
    return lax.ppermute(block, "expert", [(i, i ^ (count // 2)) for i in range(count)])


def tie(value, *others):
    return lax.optimization_barrier((value,) + others)[0]


def tie_all(values, *others):
    return lax.optimization_barrier(tuple(values) + others)[: len(values)]


def ordered_dot(y_pos, left, right, units, unit, sizes):
    rows, depth = left.shape
    width = right.shape[1]
    taken = len(units) * unit
    per_block = rows // (4 * unit)
    tile = 512

    def body(pos, left_ref, right_ref, *refs):
        outs, ordered = refs[:-1], refs[-1]

        @pl.when(pl.program_id(0) == 0)
        def _():
            for place, (step, part) in enumerate(units):
                at = (lax.rem(pos[0] + step, 4) * per_block + part) * unit
                ordered[place * unit : (place + 1) * unit, :] = left_ref[
                    pl.ds(pl.multiple_of(at, unit), unit), :
                ]

        product = dot(ordered[...], right_ref[...]).astype(BF)
        start = 0
        for out in outs:
            out[...] = product[start : start + out.shape[0], :]
            start += out.shape[0]

    return pl.pallas_call(
        body,
        out_shape=[pltpu.HBM((size, width), BF) for size in sizes],
        grid_spec=pltpu.PrefetchScalarGridSpec(
            num_scalar_prefetch=1,
            grid=(width // tile,),
            in_specs=[
                pl.BlockSpec((rows, depth), lambda i, pos: (0, 0)),
                pl.BlockSpec((depth, tile), lambda i, pos: (0, i)),
            ],
            out_specs=[pl.BlockSpec((size, tile), lambda i, pos: (0, i)) for size in sizes],
            scratch_shapes=[pltpu.VMEM((taken, depth), BF)],
        ),
        compiler_params=pltpu.CompilerParams(vmem_limit_bytes=16 << 20),
        cost_estimate=pl.CostEstimate(
            flops=2 * taken * depth * width,
            bytes_accessed=2 * (rows * depth + depth * width + taken * width),
            transcendentals=0,
        ),
    )(y_pos.reshape(1), left, pltpu.with_memory_space_constraint(right, pltpu.HBM))


def gathered_dot(y_pos, parts, right, keep):
    rows, depth = parts[0].shape
    width = right.shape[0]
    total = 4 * rows
    mid = rows // 2

    def body(pos, *refs):
        w_ref, out, full = refs[len(parts) :]
        for (step, offset), ref in zip(((0, 0), (3, 0), (1, 0), (2, 0), (2, mid)), refs[: len(parts)]):
            at = lax.rem(pos[0] + step, 4) * rows + offset
            full[pl.ds(pl.multiple_of(at, mid), ref.shape[0]), :] = ref[...]
        out[...] = dot(full[...], w_ref[...], 1, 1).astype(BF)

    vmem = pl.BlockSpec(memory_space=pltpu.VMEM)
    out_shape = [pltpu.HBM((total, width), BF)]
    out_specs = [pl.BlockSpec((total, width), lambda k: (0, 0))]
    scratch = []
    if keep:
        out_shape.append(pltpu.HBM((total, depth), BF))
        out_specs.append(pl.BlockSpec((total, depth), lambda k: (0, 0)))
    else:
        scratch.append(pltpu.VMEM((total, depth), BF))
    return pl.pallas_call(
        body,
        out_shape=out_shape,
        grid=(1,),
        in_specs=[pl.BlockSpec(memory_space=pltpu.SMEM)] + [vmem] * (len(parts) + 1),
        out_specs=out_specs,
        scratch_shapes=scratch,
        compiler_params=pltpu.CompilerParams(vmem_limit_bytes=24 << 20),
        cost_estimate=pl.CostEstimate(
            flops=2 * total * depth * width,
            bytes_accessed=2 * (total * depth + depth * width + total * width),
            transcendentals=0,
        ),
    )(y_pos.reshape(1), *parts, right)


RING_FIRST = ((2, 0), (1, 1), (2, 1), (3, 0))
RING_REST = ((0, 0), (0, 1), (1, 0), (3, 1))


def ring_sum(to_right, to_left, rest, chips):
    rows = rest.shape[0] // 4
    own_top, own_low, pass_right, pass_left = (rest[i * rows :][:rows] for i in range(4))
    from_left = chip_shift(to_right, 1)
    from_right = chip_shift(to_left, chips - 1)
    on_right = (pass_right.astype(F32) + from_left[:rows].astype(F32)).astype(BF)
    on_left = (pass_left.astype(F32) + from_right[:rows].astype(F32)).astype(BF)
    on_right, on_left = lax.optimization_barrier((on_right, on_left))
    far_left = chip_shift(on_right, 1)
    far_right = chip_shift(on_left, chips - 1)
    top = own_top.astype(F32) + from_right[rows:].astype(F32) + far_left.astype(F32)
    low = own_low.astype(F32) + from_left[rows:].astype(F32) + far_right.astype(F32)
    return jnp.concatenate([top, low])


def direct_gather(shard):
    came = {}
    for step in (2, 1, 3):
        came[step] = chip_shift(shard, step)
    return shard, came[1], came[3], came[2]


def ring_gather(shard, chips):
    mid = shard.shape[0] // 2
    left = chip_shift(shard, 1)
    right = chip_shift(shard, chips - 1)
    far_top = chip_shift(left[:mid], 1)
    far_low = chip_shift(right[mid:], chips - 1)
    return shard, left, right, far_top, far_low


def pair_rows(block):
    far = core_swap(block)
    return jnp.concatenate([block, far], axis=0)


def join_weights(gate_own, up_own, gate_far, up_far):
    rows, units = gate_own.shape
    steps = 4
    block = rows // steps

    def body(gate_a, up_a, gate_b, up_b, out):
        first = pl.program_id(0) < steps

        @pl.when(first)
        def _():
            out[:, :units] = gate_a[...]
            out[:, units:] = up_a[...]

        @pl.when(jnp.logical_not(first))
        def _():
            out[:, :units] = gate_b[...]
            out[:, units:] = up_b[...]

    near = pl.BlockSpec((block, units), lambda i: (jnp.minimum(i, steps - 1), 0))
    far = pl.BlockSpec((block, units), lambda i: (jnp.maximum(i - steps, 0), 0))
    moved = 8 * rows * units
    return pl.pallas_call(
        body,
        out_shape=pltpu.HBM((2 * rows, 2 * units), gate_own.dtype),
        grid=(2 * steps,),
        in_specs=[near, near, far, far],
        out_specs=pl.BlockSpec((block, 2 * units), lambda i: (i, 0)),
        compiler_params=pltpu.CompilerParams(vmem_limit_bytes=8 << 20),
        cost_estimate=pl.CostEstimate(flops=0, bytes_accessed=2 * moved, transcendentals=0),
    )(gate_own, up_own, gate_far, up_far)


def pair_sum(partial):
    split = partial.shape[0] // 2
    far = core_swap(partial[split:].astype(BF))
    return partial[:split] + far.astype(F32)


def shards(
    tokens,
    cotangent,
    slot_tokens,
    slot_counts,
    slot_gates,
    swap_pairs,
    gate_weight,
    up_weight,
    down_weight,
    first_moment,
    second_moment,
):
    tok_count, model_cols = tokens.shape
    experts = slot_counts.shape[1]
    capacity = slot_tokens.shape[2]
    own_slots = capacity // 2
    rows = experts * own_slots
    pair_cols = 2 * model_cols
    chips = lax.axis_size("dp") // 2
    dp_pos = lax.axis_index("dp")
    core, y_pos = dp_pos % 2, dp_pos // 2
    position = lax.axis_index("expert")
    half_count = swap_pairs.shape[0]
    own_swap = (
        jnp.sum(jnp.where(jnp.arange(half_count) == position % half_count, swap_pairs, 0)) > 0
    )

    def own_part(table):
        return lax.dynamic_slice_in_dim(table, core * own_slots, own_slots, 1)

    live = (own_part(jnp.arange(capacity)[None, :]) < slot_counts[0][:, None]).reshape(-1)
    route = own_part(slot_tokens[0]).reshape(-1)
    weighted = jnp.where(live, own_part(slot_gates[0]).reshape(-1), 0.0)
    masked_route = jnp.where(live, route, -1)
    token_ids = jnp.arange(tok_count)

    def exchange(block):
        return lax.all_to_all(
            block.reshape(experts, own_slots, pair_cols), "expert", 0, 0, tiled=True
        ).reshape(rows, pair_cols)

    token_cols = pair_rows(tokens.T)
    pick = (masked_route[:, None] == token_ids[None, :]).astype(BF)
    arrived = exchange(dot(pick, token_cols, 1, 1).astype(BF))
    grad_cols = pair_rows(cotangent.T)
    grad_rows = (dot(pick, grad_cols, 1, 1) * weighted[:, None]).astype(BF)
    far_gate = core_swap(gate_weight[0])
    far_up = core_swap(up_weight[0])
    gate_up = join_weights(gate_weight[0], up_weight[0], far_gate, far_up)
    down_cols = pair_rows(down_weight[0].T)
    moment_one = first_moment[0].T
    moment_two = second_moment[0].T
    far_one = expert_swap(tie(moment_one, grad_cols).astype(BF))
    far_two = expert_swap(tie(moment_two, grad_cols).astype(BF))

    arrived, gate_up, down_cols, grad_rows = lax.optimization_barrier(
        (arrived, gate_up, down_cols, grad_rows)
    )
    arrived_grad = exchange(grad_rows)
    hidden_units = down_weight.shape[1]
    half = rows // (2 * chips)
    sent = ordered_dot(y_pos, arrived, gate_up, RING_FIRST, half, (2 * half, 2 * half))
    (kept,) = ordered_dot(y_pos, arrived, gate_up, RING_REST, half, (4 * half,))
    preact = ring_sum(*sent, kept, chips)
    gate_pre, up_pre = preact[:, :hidden_units], preact[:, hidden_units:]
    sig = jax.nn.sigmoid(gate_pre)
    hidden_shard = (gate_pre * sig * up_pre).astype(BF)
    arrived_grad = tie(arrived_grad, hidden_shard)
    terms = ordered_dot(
        y_pos, arrived_grad, down_cols, ((2, 0), (1, 0), (3, 0), (0, 0)), 2 * half, (2 * half,) * 4
    )
    gathered = direct_gather(hidden_shard)
    gathered = tie_all(gathered, *terms)
    out_rows, hidden = gathered_dot(y_pos, gathered, down_cols, True)
    returned = exchange(out_rows)

    hidden_grad = terms[3].astype(F32)
    for step, term in zip((2, 1, 3), terms):
        came = chip_shift(term, step)
        hidden_grad = hidden_grad + came.astype(F32)
    gate_grad = hidden_grad * up_pre * sig * (1.0 + gate_pre * (1.0 - sig))
    up_grad = hidden_grad * gate_pre * sig
    pre_shard = jnp.concatenate([gate_grad, up_grad], axis=1).astype(BF)
    weight_grad = pair_sum(dot(tie(arrived_grad, pre_shard), hidden, 0, 0))
    sent_grad = weight_grad.astype(BF)
    gathered = ring_gather(pre_shard, chips)
    gathered = tie_all(gathered, sent_grad)
    far_grad = expert_swap(sent_grad)
    (back,) = gathered_dot(y_pos, gathered, gate_up, False)
    returned_grad = exchange(back)

    one = jnp.where(own_swap, far_one.astype(F32), moment_one)
    two = jnp.where(own_swap, far_two.astype(F32), moment_two)
    grad = jnp.where(own_swap, far_grad.astype(F32), weight_grad)
    new_one = beta_first * one + (1.0 - beta_first) * grad
    new_two = beta_second * two + (1.0 - beta_second) * grad * grad
    step_dir = (new_one / (jnp.sqrt(new_two) + adam_eps)).astype(BF)

    match = masked_route[:, None] == token_ids[None, :]
    top = lax.reduce_precision(weighted, 8, 7)
    rest = weighted - top
    mixed = pair_sum(
        dot(returned, jnp.where(match, top[:, None], 0.0).astype(BF), 0, 0)
        + dot(returned, jnp.where(match, rest[:, None], 0.0).astype(BF), 0, 0),
    ).astype(BF)
    returned_grad = tie(returned_grad, mixed, step_dir)
    token_grad = pair_sum(dot(returned_grad, match.astype(BF), 0, 0)).astype(BF)
    return (mixed.T, token_grad.T, new_one.T[None], new_two.T[None], step_dir.T[None])


def solution(mesh):
    return jax.shard_map(
        shards,
        mesh=mesh,
        in_specs=(
            P("expert", "dp"),
            P("expert", "dp"),
            P("expert", None, None),
            P("expert", None),
            P("expert", None, None),
            P(),
            P("expert", "dp", None),
            P("expert", "dp", None),
            P("expert", None, "dp"),
            P("expert", None, "dp"),
            P("expert", None, "dp"),
        ),
        out_specs=(
            P("expert", "dp"),
            P("expert", "dp"),
            P("expert", None, "dp"),
            P("expert", None, "dp"),
            P("expert", None, "dp"),
        ),
        check_vma=False,
    )
```
